512 devices in a mesh: dp: 64 (over z_lo, x, y), tm: 8 (over z_hi, core).
Axes of the slice: x: 4, y: 8, z: 8 (z_hi: 4, z_lo: 2; z = z_hi * 2 + z_lo), core: 2. Of those that a mesh axis runs over, the one named last changes fastest.
Arguments:
- frames: bfloat16 [65536, 1024], P(('dp', 'tm')), may hold values from -40 to 40
- out_grad: bfloat16 [65536, 1024], P(('dp', 'tm')), may hold values from -0.0625 to 0.0625
- norm1_gain: float32 [1024], replicated, may hold values from 0.25 to 1.75
- w_query: bfloat16 [1024, 512], replicated, may hold values from -0.1875 to 0.1875
- w_kv: bfloat16 [1024, 1024], replicated, may hold values from -0.1875 to 0.1875
- w_out: bfloat16 [512, 1024], replicated, may hold values from -0.25 to 0.25
- norm2_gain: float32 [1024], replicated, may hold values from 0.25 to 1.75
- conv_kernel: float32 [31, 1024], replicated, may hold values from -1 to 1
- conv_bias: float32 [1024], replicated, may hold values from -3 to 3
- utt_blocks: int32 [64, 4], P('dp'), may hold values from 1 to 10, 16 in all within a row
- block_slot: int32 [64, 16], P('dp'), may hold values from 0 to 15, each once within a row
- left_count: int32 [64, 16], P('dp'), may hold values from 0 to 2
Outputs:
- layer_out: bfloat16 [65536, 1024], P(('dp', 'tm'))
- kv_grad: float32 [1024, 1024], P('dp', 'tm')
The draws below stay inside these ranges and needn't reach their ends.
Inputs may be any that keep to these rules, and one draw needn't show every extreme that they name: `utt_blocks`: the 4 lengths of a group add up to 16. `block_slot`: each group's row names every slot once; slot s lies on index s // 2 of tm.
All inputs are finite; a program needn't handle non-finite values.
Results may differ from the reference program's by a relative error of at most 0.018.
Values may be sent and summed in bfloat16 or wider, within the bound.
A program may use at most 64 MiB of HBM per device.

```python
import math
import jax
import jax.numpy as jnp
import numpy as np
from jax import lax

D = 1024
HEADS = 8
HD = 64
KERNEL = 31
BLOCK = 64
LC = 2
HQ = 512
KVW = 1024
BLOCKS = 16
UTT = 4
MOST = 10
ROWS = 65536
N_DP = 64


def draw_frames(key, part):
    first_key, second_key, third_key = jax.random.split(key, 3)
    row_scale = jnp.exp(jax.random.uniform(first_key, (ROWS, 1), jnp.float32, -1.15, 1.15))
    col_scale = jnp.exp(jax.random.uniform(second_key, (1, D), jnp.float32, -1.15, 1.15))
    noise = jnp.clip(jax.random.normal(third_key, (ROWS, D), jnp.float32), -4.0, 4.0)
    return (noise * row_scale * col_scale).astype(jnp.bfloat16)


def with_ends(result, stream_key, least, largest):
    dims = result.shape
    index_at = [jax.random.randint(jax.random.fold_in(stream_key, axis), (), 0, dims[axis]) for axis in range(len(dims))]
    result = result.at[tuple(index_at)].set(least)
    longest = dims.index(max(dims))
    index_at[longest] = (index_at[longest] + 1) % dims[longest]
    return result.at[tuple(index_at)].set(largest)


def shard_levels(stream_key, extent, cuts, low, high):
    factor_of, own = 1.0, jax.random.fold_in(stream_key, 6)
    for axis_at, shards_of in cuts:
        heights = jnp.exp(jax.random.uniform(jax.random.fold_in(own, axis_at), (shards_of,), jnp.float32, low / len(cuts), high / len(cuts)))
        factor_of = factor_of * jnp.repeat(heights, extent[axis_at] // shards_of).reshape([-1 if axis == axis_at else 1 for axis in range(len(extent))])
    return factor_of


def split_up(count, total, most, lean):
    portions = [(1 << 20) // math.isqrt(rank ** lean) + 1 for rank in range(2, count + 1)]
    surplus, given = total - most - (count - 1), [1] * (count - 1)
    while surplus > 0:
        free = [i for i in range(count - 1) if given[i] < most]
        mass, budget = sum([portions[i] for i in free]), surplus
        for i in free:
            more = min(most - given[i], max(1, budget * portions[i] // mass), surplus)
            given[i] = given[i] + more
            surplus = surplus - more
    return np.array([most] + given)


def ragged_sizes(own_key, count, total, limit, lean):
    if count == 2:
        one = jax.random.randint(own_key, (), max(1, total - limit), min(limit, total - 1) + 1)
        return jnp.stack([one, total - one])
    sizes = jnp.asarray(split_up(count, total, limit, lean), jnp.int32)
    couples = (count - 1) // 2
    donor, taker = sizes[1:1 + 2 * couples:2], sizes[2:2 + 2 * couples:2]
    slack = jnp.minimum(donor - 1, limit - taker)
    passed = jax.random.randint(jax.random.fold_in(own_key, 1), (couples,), 0, 1 << 20) % (slack + 1)
    sizes = sizes.at[1:1 + 2 * couples:2].set(donor - passed).at[2:2 + 2 * couples:2].set(taker + passed)
    return sizes[jax.random.permutation(jax.random.fold_in(own_key, 2), count)]


def bell_draw(rng, extent, deviation, limit, cuts=(), kind=jnp.bfloat16):
    entries = deviation * jax.random.normal(rng, extent, jnp.float32)
    if cuts:
        entries = entries * shard_levels(rng, extent, cuts, -0.22, 0.18)
    return jnp.clip(entries, -limit, limit).astype(kind)


def setup_inputs(seed: int = 0) -> dict:
    keys = jax.random.split(jax.random.key(seed), 13)
    frames = draw_frames(jax.random.fold_in(keys[12], 71), 0)
    out_grad = bell_draw(keys[1], (ROWS, D), (ROWS // 9) ** -0.5, 0.0625, ((0, 512),))
    norm1_gain = jnp.clip(1.0 + 0.15 * jax.random.normal(keys[2], (D,), jnp.float32), 0.25, 1.75)
    w_query = bell_draw(keys[3], (D, HQ), D ** -0.5, 0.1875)
    w_kv = bell_draw(keys[4], (D, KVW), D ** -0.5, 0.1875)
    w_out = bell_draw(keys[5], (HQ, D), HQ ** -0.5, 0.25)
    norm2_gain = jnp.clip(1.0 + 0.15 * jax.random.normal(keys[6], (D,), jnp.float32), 0.25, 1.75)
    conv_kernel = bell_draw(keys[7], (KERNEL, D), KERNEL ** -0.5, 1.0, (), jnp.float32)
    conv_bias = bell_draw(keys[8], (D,), 0.5, 3.0, (), jnp.float32)
    utt_blocks = jax.vmap(lambda own: ragged_sizes(own, UTT, BLOCKS, MOST, 2))(jax.random.split(keys[9], N_DP)).reshape((N_DP, UTT)).astype(jnp.int32)
    block_slot = jax.vmap(lambda own: jax.random.permutation(own, BLOCKS))(jax.random.split(keys[10], N_DP)).reshape((N_DP, BLOCKS)).astype(jnp.int32)
    left_count = with_ends(jax.random.randint(keys[11], (N_DP, BLOCKS), 0, LC + 1), jax.random.fold_in(keys[11], 1), 0, LC).astype(jnp.int32)
    return {"frames": frames, "out_grad": out_grad, "norm1_gain": norm1_gain, "w_query": w_query, "w_kv": w_kv, "w_out": w_out, "norm2_gain": norm2_gain, "conv_kernel": conv_kernel, "conv_bias": conv_bias, "utt_blocks": utt_blocks, "block_slot": block_slot, "left_count": left_count}


EPSILON = 1e-05
SOFT_CAP = 4.0

def to_bf16(values):
    return lax.optimization_barrier(values.astype(jnp.bfloat16))

def norm_parts(values):
    row_mean = lax.optimization_barrier(jnp.mean(values, axis=-1, keepdims=True))
    centred = values - row_mean
    scale_inv = lax.rsqrt(lax.optimization_barrier(jnp.mean(centred * centred, axis=-1, keepdims=True)) + EPSILON)
    return (centred * scale_inv, scale_inv)

def norm_back(grad_in, unit_rows, scale_inv, gain_row):
    scaled = grad_in * gain_row
    first_mean = lax.optimization_barrier(jnp.mean(scaled, axis=-1, keepdims=True))
    second_mean = lax.optimization_barrier(jnp.mean(scaled * unit_rows, axis=-1, keepdims=True))
    return scale_inv * (scaled - first_mean - unit_rows * second_mean)

def block_layout(lengths, counts, block_total):
    utter_ends = jnp.cumsum(lengths).astype(jnp.int32)
    utter_starts = (utter_ends - lengths).astype(jnp.int32)
    block_index = jnp.arange(block_total, dtype=jnp.int32)
    past_end = block_index[:, None] >= utter_ends[None, :]
    utterance = lax.optimization_barrier(jnp.sum(past_end.astype(jnp.int32), axis=1))
    matches = utterance[:, None] == jnp.arange(lengths.shape[0], dtype=jnp.int32)[None, :]
    first_block = lax.optimization_barrier(jnp.sum(jnp.where(matches, utter_starts[None, :], 0), axis=1)).astype(jnp.int32)
    position = (block_index - first_block).astype(jnp.int32)
    return (position, jnp.minimum(counts, position).astype(jnp.int32))

def attend(queries, keys_values, allowed):
    block_count, row_count, query_width = queries.shape
    query_heads = queries.astype(jnp.float32).reshape(block_count, row_count, HEADS, HD)
    key_heads = keys_values[..., :query_width].astype(jnp.float32).reshape(block_count, -1, HEADS, HD)
    value_heads = keys_values[..., query_width:].astype(jnp.float32).reshape(block_count, -1, HEADS, HD)
    raw_scores = jnp.einsum('nrhd,nkhd->nhrk', query_heads, key_heads)
    capped = SOFT_CAP * jnp.tanh(raw_scores / (SOFT_CAP * math.sqrt(HD)))
    exped = jnp.where(allowed[:, None], jnp.exp(capped), 0.0)
    attn_probs = exped / lax.optimization_barrier(jnp.sum(exped, axis=-1, keepdims=True))
    probs_b = to_bf16(attn_probs).astype(jnp.float32)
    context = jnp.einsum('nhrk,nkhd->nrhd', probs_b, value_heads)
    return (to_bf16(context).reshape(block_count, row_count, query_width), attn_probs, capped)

def attend_back(queries, keys_values, context, attn_probs, capped, grad_context):
    block_count, row_count, query_width = queries.shape
    query_heads = queries.astype(jnp.float32).reshape(block_count, row_count, HEADS, HD)
    value_heads = keys_values[..., query_width:].astype(jnp.float32).reshape(block_count, -1, HEADS, HD)
    grad_heads = grad_context.astype(jnp.float32).reshape(block_count, row_count, HEADS, HD)
    context_heads = context.astype(jnp.float32).reshape(block_count, row_count, HEADS, HD)
    grad_probs = jnp.einsum('nrhd,nkhd->nhrk', grad_heads, value_heads)
    delta_rows = jnp.transpose(lax.optimization_barrier(jnp.sum(grad_heads * context_heads, axis=-1)), (0, 2, 1))[..., None]
    grad_raw = attn_probs * (grad_probs - delta_rows) * (1.0 - (capped / SOFT_CAP) ** 2) / math.sqrt(HD)
    grad_raw_b = to_bf16(grad_raw).astype(jnp.float32)
    probs_b = to_bf16(attn_probs).astype(jnp.float32)
    key_part = jnp.einsum('nhrk,nrhd->nkhd', grad_raw_b, query_heads)
    value_part = jnp.einsum('nhrk,nrhd->nkhd', probs_b, grad_heads)
    key_rows = key_part.shape[1]
    joined = jnp.concatenate([key_part.reshape(block_count, key_rows, query_width), value_part.reshape(block_count, key_rows, query_width)], axis=-1)
    return to_bf16(joined)

def group_pass(frames, out_grad, lengths, slot_table, counts, norm1_gain, w_query, w_kv, w_out, norm2_gain, conv_kernel, conv_bias):
    block_total = slot_table.shape[0]
    tail_rows = KERNEL - 1
    span_blocks = LC + 1
    block_index = jnp.arange(block_total, dtype=jnp.int32)
    position, reach = block_layout(lengths, counts, block_total)
    in_blocks = jnp.take(frames.reshape(block_total, BLOCK, D), slot_table, axis=0)
    grad_blocks = jnp.take(out_grad.reshape(block_total, BLOCK, D), slot_table, axis=0)
    unit_first, unused_inv = norm_parts(in_blocks.astype(jnp.float32))
    normed = to_bf16(unit_first * norm1_gain)
    flat_normed = normed.reshape(block_total * BLOCK, D)
    queries = to_bf16(jnp.dot(flat_normed, w_query, preferred_element_type=jnp.float32)).reshape(block_total, BLOCK, HQ)
    keys_values = to_bf16(jnp.dot(flat_normed, w_kv, preferred_element_type=jnp.float32)).reshape(block_total, BLOCK, KVW)
    window = jnp.maximum(block_index[:, None] - LC + jnp.arange(span_blocks, dtype=jnp.int32)[None, :], 0).astype(jnp.int32)
    kv_window = jnp.take(keys_values, window, axis=0).reshape(block_total, span_blocks * BLOCK, KVW)
    block_ok = jnp.arange(span_blocks, dtype=jnp.int32)[None, :] >= LC - reach[:, None]
    allowed = jnp.broadcast_to(jnp.repeat(block_ok, BLOCK, axis=1)[:, None, :], (block_total, BLOCK, span_blocks * BLOCK))
    context, attn_probs, capped = attend(queries, kv_window, allowed)
    hidden = in_blocks.astype(jnp.float32) + jnp.dot(context.reshape(-1, HQ), w_out, preferred_element_type=jnp.float32).reshape(block_total, BLOCK, D)
    unit_second, inv_second = norm_parts(hidden)
    conv_in = to_bf16(unit_second * norm2_gain)
    prev_block = jnp.maximum(block_index - 1, 0).astype(jnp.int32)
    has_prev = position >= 1
    cache_rows = jnp.where(has_prev[:, None, None], jnp.take(conv_in, prev_block, axis=0)[:, BLOCK - tail_rows:], jnp.zeros((), jnp.bfloat16))
    extended = jnp.concatenate([cache_rows, conv_in], axis=1).astype(jnp.float32)
    mixed_conv = conv_bias + conv_kernel[0] * extended[:, :BLOCK]
    for tap_index in range(1, KERNEL):
        mixed_conv = mixed_conv + conv_kernel[tap_index] * extended[:, tap_index:tap_index + BLOCK]
    gate_value = jax.nn.sigmoid(mixed_conv)
    layer_out = (hidden + mixed_conv * gate_value).astype(jnp.bfloat16)
    out_grad_f = grad_blocks.astype(jnp.float32)
    grad_mixed = out_grad_f * gate_value * (1.0 + mixed_conv * (1.0 - gate_value))
    padded = jnp.pad(grad_mixed, ((0, 0), (tail_rows, tail_rows), (0, 0)))
    grad_ext = conv_kernel[0] * padded[:, tail_rows:tail_rows + BLOCK + tail_rows]
    for tap_index in range(1, KERNEL):
        grad_ext = grad_ext + conv_kernel[tap_index] * padded[:, tail_rows - tap_index:tail_rows - tap_index + BLOCK + tail_rows]
    carried = jnp.where(has_prev[:, None, None], grad_ext[:, :tail_rows], 0.0)
    grad_hidden = out_grad_f + norm_back(grad_ext[:, tail_rows:], unit_second, inv_second, norm2_gain)
    grad_carried = norm_back(carried, jnp.take(unit_second, prev_block, axis=0)[:, BLOCK - tail_rows:], jnp.take(inv_second, prev_block, axis=0)[:, BLOCK - tail_rows:], norm2_gain)
    grad_ctx_own = to_bf16(jnp.dot(to_bf16(grad_hidden).reshape(-1, D), w_out.T, preferred_element_type=jnp.float32)).reshape(block_total, BLOCK, HQ)
    grad_ctx_carried = to_bf16(jnp.dot(to_bf16(grad_carried).reshape(-1, D), w_out.T, preferred_element_type=jnp.float32)).reshape(block_total, tail_rows, HQ)
    term_own = attend_back(queries, kv_window, context, attn_probs, capped, grad_ctx_own)
    term_carried = attend_back(jnp.take(queries, prev_block, axis=0)[:, BLOCK - tail_rows:], jnp.take(kv_window, prev_block, axis=0), jnp.take(context, prev_block, axis=0)[:, BLOCK - tail_rows:], jnp.take(attn_probs, prev_block, axis=0)[:, :, BLOCK - tail_rows:], jnp.take(capped, prev_block, axis=0)[:, :, BLOCK - tail_rows:], grad_ctx_carried)
    normed_window = jnp.take(normed, window, axis=0).reshape(block_total, span_blocks * BLOCK, D).astype(jnp.float32)
    group_grad = jnp.einsum('nkd,nke->de', normed_window, term_own.astype(jnp.float32))
    group_grad = group_grad + jnp.einsum('nkd,nke->de', jnp.take(normed_window, prev_block, axis=0), term_carried.astype(jnp.float32))
    out_slots = jnp.zeros_like(layer_out).at[slot_table].set(layer_out)
    return (out_slots.reshape(block_total * BLOCK, D), group_grad)

def reference(frames, out_grad, norm1_gain, w_query, w_kv, w_out, norm2_gain, conv_kernel, conv_bias, utt_blocks, block_slot, left_count):
    group_total = utt_blocks.shape[0]
    group_rows = frames.shape[0] // group_total
    frames_grouped = frames.reshape(group_total, group_rows, D)
    grads_grouped = out_grad.reshape(group_total, group_rows, D)

    def step(running, item):
        frame_rows, grad_rows, lengths, slot_table, counts = item
        out_rows, group_grad = group_pass(frame_rows, grad_rows, lengths, slot_table, counts, norm1_gain, w_query, w_kv, w_out, norm2_gain, conv_kernel, conv_bias)
        return (running + group_grad, out_rows)
    start_grad = jnp.zeros((D, KVW), jnp.float32)
    kv_grad, outputs = lax.scan(step, start_grad, (frames_grouped, grads_grouped, utt_blocks, block_slot, left_count))
    return (outputs.reshape(frames.shape[0], D), kv_grad)
```

```python
import jax
import jax.numpy as jnp
from jax import lax
from jax.experimental import pallas as pl
from jax.experimental.pallas import tpu as pltpu
from jax.sharding import PartitionSpec as P

HEADS = 8
HEAD = 64
PAIRS = HEADS // 2
TAPS = 31
BLOCK = 64
BLOCKS = 16
TIME = 8
UTTERANCES = 4
WIDTH = 1024
QUERY = 512
KEYVAL = 1024
LANES = 128
TAIL = 32
ROWS = TAIL + BLOCK
SPAN = 4 * BLOCK
NX, NY, NZ_LO, NZ_HI = 4, 8, 2, 4
EPSILON = 1e-05
SOFT_CAP = 4.0
MESH = pl.DeviceIdType.MESH
F32 = jnp.float32
BF16 = jnp.bfloat16


def send(src, dst, send_sem, recv_sem, dp, tm):
    return pltpu.make_async_remote_copy(
        src_ref=src,
        dst_ref=dst,
        send_sem=send_sem,
        recv_sem=recv_sem,
        device_id=(dp, tm),
        device_id_type=MESH,
    )


def greet(partners):
    barrier = pltpu.get_barrier_semaphore()
    for dp, tm in partners:
        pl.semaphore_signal(barrier, inc=1, device_id=(dp, tm), device_id_type=MESH)
    pl.semaphore_wait(barrier, len(partners))


def gather_kernel(frames_ref, gath_ref, send_sem, recv_sem, own_sem):
    dp = lax.axis_index("dp")
    tm = lax.axis_index("tm")
    z_hi, core = tm // 2, tm % 2
    up = ((z_hi + 1) % NZ_HI) * 2 + core
    down = ((z_hi + NZ_HI - 1) % NZ_HI) * 2 + core
    far = ((z_hi + 2) % NZ_HI) * 2 + core
    sibling = z_hi * 2 + 1 - core
    greet([(dp, up), (dp, down), (dp, sibling)])

    def own(block):
        return frames_ref.at[pl.ds(block * BLOCK, BLOCK)]

    def put(src, slot, target, number):
        copy = send(
            src, gath_ref.at[slot], send_sem.at[number], recv_sem.at[slot], dp, target
        )
        copy.start()
        return copy

    def landed(slot):
        send(
            gath_ref.at[slot],
            gath_ref.at[slot],
            send_sem.at[0],
            recv_sem.at[slot],
            dp,
            sibling,
        ).wait_recv()

    copies = [
        put(own(0), 2 * tm, up, 0),
        put(own(1), 2 * tm + 1, down, 1),
        put(own(1), 2 * tm + 1, up, 2),
        put(own(0), 2 * tm, down, 3),
        put(own(0), 2 * tm, sibling, 4),
        put(own(1), 2 * tm + 1, sibling, 5),
    ]
    locals_ = [
        pltpu.make_async_copy(own(b), gath_ref.at[2 * tm + b], own_sem.at[b])
        for b in range(2)
    ]
    for copy in locals_:
        copy.start()
    slot = 2 * down
    landed(slot)
    copies.append(put(gath_ref.at[slot], slot, up, 6))
    copies.append(put(gath_ref.at[slot], slot, sibling, 8))
    slot = 2 * up + 1
    landed(slot)
    copies.append(put(gath_ref.at[slot], slot, down, 7))
    copies.append(put(gath_ref.at[slot], slot, sibling, 9))
    for number, slot in enumerate((2 * down + 1, 2 * up, 2 * far, 2 * far + 1)):
        landed(slot)
        copies.append(put(gath_ref.at[slot], slot, sibling, 10 + number))
    for other in (sibling, up + 1 - 2 * core, down + 1 - 2 * core, far + 1 - 2 * core):
        for b in range(2):
            landed(2 * other + b)
    for copy in locals_:
        copy.wait()
    for copy in copies:
        copy.wait_send()


def gather_frames(frames):
    return pl.pallas_call(
        gather_kernel,
        out_shape=jax.ShapeDtypeStruct((BLOCKS, BLOCK, WIDTH), BF16),
        in_specs=[pl.BlockSpec(memory_space=pltpu.VMEM)],
        out_specs=pl.BlockSpec(memory_space=pltpu.VMEM),
        scratch_shapes=[
            pltpu.SemaphoreType.DMA((14,)),
            pltpu.SemaphoreType.DMA((BLOCKS,)),
            pltpu.SemaphoreType.DMA((2,)),
        ],
        compiler_params=pltpu.CompilerParams(
            collective_id=0, has_side_effects=True, vmem_limit_bytes=16 << 20
        ),
        name="gather_frames",
    )(frames)


def unit_rows(rows):
    row_mean = jnp.mean(rows, axis=-1, keepdims=True)
    centred = rows - row_mean
    inv = lax.rsqrt(jnp.mean(centred * centred, axis=-1, keepdims=True) + EPSILON)
    return centred * inv, inv


def dot(a, b, dims):
    return lax.dot_general(a, b, (dims, ((), ())), preferred_element_type=F32)


def stack_heads(pair_rows):
    lane = lax.broadcasted_iota(jnp.int32, pair_rows.shape, 1)
    zero = jnp.zeros((), pair_rows.dtype)
    return jnp.concatenate(
        [
            jnp.where(lane < HEAD, pair_rows, zero),
            jnp.where(lane >= HEAD, pair_rows, zero),
        ],
        axis=0,
    )


def local_kernel(
    lengths_ref,
    slots_ref,
    counts_ref,
    gath_ref,
    grad_ref,
    gain1_ref,
    w_query_ref,
    w_kv_ref,
    w_out_ref,
    gain2_ref,
    taps_ref,
    bias_ref,
    out_ref,
    parts_ref,
    normed_ref,
    kv_ref,
    query_ref,
    rows_ref,
    probs_ref,
    slope_ref,
    context_ref,
    hidden_ref,
    unit_ref,
    inv_ref,
    conv_ref,
    pad_ref,
    back_ref,
    grad_context_ref,
    term_ref,
):
    tm = lax.axis_index("tm")

    def position(block):
        end, start = jnp.int32(0), jnp.int32(0)
        for u in range(UTTERANCES):
            length = lengths_ref[0, u]
            end = end + length
            start = start + jnp.where(block >= end, length, 0)
        return block - start

    blocks = []
    for i in range(2):
        block = jnp.int32(0)
        for b in range(BLOCKS):
            block = block + jnp.where(slots_ref[0, b] == 2 * tm + i, b, 0)
        before = jnp.maximum(block - 1, 0)
        at, at_before = position(block), position(before)
        reach = jnp.minimum(counts_ref[0, block], at)
        reach_before = jnp.minimum(counts_ref[0, before], at_before)
        window = [slots_ref[0, jnp.maximum(block - 3 + lane, 0)] for lane in range(4)]
        blocks.append((reach, reach_before, at >= 1, window))

    gain1 = gain1_ref[...]
    for i in range(2):
        for lane in range(4):
            rows = gath_ref[blocks[i][3][lane]].astype(F32)
            unit, _ = unit_rows(rows)
            normed_ref[i * SPAN + lane * BLOCK : i * SPAN + (lane + 1) * BLOCK] = (
                unit * gain1
            ).astype(BF16)
            if lane == 2:
                rows_ref[i * ROWS : i * ROWS + TAIL] = rows[BLOCK - TAIL :]
            if lane == 3:
                rows_ref[i * ROWS + TAIL : (i + 1) * ROWS] = rows
        queries = dot(
            normed_ref[(i + 1) * SPAN - ROWS : (i + 1) * SPAN],
            w_query_ref[...],
            ((1,), (0,)),
        )
        query_ref[i * ROWS : (i + 1) * ROWS] = queries.astype(BF16)
    kv_ref[...] = dot(normed_ref[...], w_kv_ref[...], ((1,), (0,))).astype(BF16)

    key_lane = lax.broadcasted_iota(jnp.int32, (ROWS, SPAN), 1) // BLOCK
    row = lax.broadcasted_iota(jnp.int32, (ROWS, SPAN), 0)
    for i in range(2):
        reach, reach_before, _, _ = blocks[i]
        last = jnp.where(row < TAIL, 2, 3)
        first = last - jnp.where(row < TAIL, reach_before, reach)
        allowed = jnp.where((key_lane >= first) & (key_lane <= last), 1.0, 0.0)
        allowed = jnp.concatenate([allowed, allowed], axis=0)
        for pair in range(PAIRS):
            columns = slice(pair * LANES, (pair + 1) * LANES)
            value_columns = slice(QUERY + pair * LANES, QUERY + (pair + 1) * LANES)
            span = slice(i * SPAN, (i + 1) * SPAN)
            q = stack_heads(query_ref[i * ROWS : (i + 1) * ROWS, columns])
            raw = dot(q, kv_ref[span, columns], ((1,), (1,)))
            bent = jnp.tanh(raw * (1.0 / (SOFT_CAP * 8.0)))
            exped = jnp.exp(SOFT_CAP * bent) * allowed
            probs = exped / jnp.sum(exped, axis=-1, keepdims=True)
            probs_b = probs.astype(BF16)
            probs_ref[i * PAIRS + pair] = probs_b
            slope_ref[i * PAIRS + pair] = probs * (1.0 - bent * bent) * 0.125
            both = dot(probs_b, kv_ref[span, value_columns], ((1,), (0,)))
            lane = lax.broadcasted_iota(jnp.int32, (ROWS, LANES), 1)
            context_ref[i * ROWS : (i + 1) * ROWS, columns] = jnp.where(
                lane < HEAD, both[:ROWS], both[ROWS:]
            ).astype(BF16)

    gain2 = gain2_ref[...]
    projected = dot(context_ref[...], w_out_ref[...], ((1,), (0,)))
    hidden_ref[...] = rows_ref[...] + projected
    for i in range(2):
        has_prev = blocks[i][2]
        span = slice(i * ROWS, (i + 1) * ROWS)
        unit, inv = unit_rows(hidden_ref[span])
        unit_ref[span] = unit
        inv_ref[span] = jnp.broadcast_to(inv, (ROWS, LANES))
        conv_in = (unit * gain2).astype(BF16).astype(F32)
        keep = jnp.where(has_prev, 1.0, 0.0)
        conv_ref[i * ROWS : i * ROWS + TAIL] = conv_in[:TAIL] * keep
        conv_ref[i * ROWS + TAIL : (i + 1) * ROWS] = conv_in[TAIL:]

    pad_ref[...] = jnp.zeros_like(pad_ref)
    for i in range(2):
        keep = jnp.where(blocks[i][2], 1.0, 0.0)

        def strip_pass(strip, carry):
            lanes = pl.ds(pl.multiple_of(strip * LANES, LANES), LANES)
            ext = conv_ref[i * ROWS : (i + 1) * ROWS, lanes]
            mixed = jnp.broadcast_to(bias_ref[:, lanes], (BLOCK, LANES))
            for shift in range(8):
                turned = (
                    ext if shift == 0 else pltpu.roll(ext, ROWS - shift, axis=0)
                )
                for base in range(0, 40, 8):
                    tap = base + shift - 2
                    if 0 <= tap < TAPS:
                        mixed = (
                            mixed
                            + taps_ref[tap : tap + 1, lanes]
                            * turned[base : base + BLOCK]
                        )
            gate = 1.0 / (1.0 + jnp.exp(-mixed))
            hidden = hidden_ref[i * ROWS + TAIL : (i + 1) * ROWS, lanes]
            out_ref[i * BLOCK : (i + 1) * BLOCK, lanes] = (
                hidden + mixed * gate
            ).astype(BF16)
            out_grad = grad_ref[i * BLOCK : (i + 1) * BLOCK, lanes].astype(F32)
            grad_mixed = out_grad * gate * (1.0 + mixed * (1.0 - gate))
            zeros = jnp.zeros((TAIL, LANES), F32)
            padded = jnp.concatenate([zeros, grad_mixed, zeros], axis=0)
            total = jnp.zeros((ROWS, LANES), F32)
            for shift in range(8):
                turned = (
                    padded
                    if shift == 0
                    else pltpu.roll(padded, ROWS + TAIL - shift, axis=0)
                )
                for base in range(0, 32, 8):
                    tap = TAPS - 1 - base - shift
                    if 0 <= tap < TAPS:
                        total = (
                            total
                            + taps_ref[tap : tap + 1, lanes]
                            * turned[base : base + ROWS]
                        )
            back_ref[i * ROWS : i * ROWS + TAIL, lanes] = total[:TAIL] * keep
            back_ref[i * ROWS + TAIL : (i + 1) * ROWS, lanes] = total[TAIL:]
            return carry

        lax.fori_loop(0, WIDTH // LANES, strip_pass, 0)

    for i in range(2):
        span = slice(i * ROWS, (i + 1) * ROWS)
        scaled = back_ref[span] * gain2
        unit = unit_ref[span]
        first = jnp.mean(scaled, axis=-1, keepdims=True)
        second = jnp.mean(scaled * unit, axis=-1, keepdims=True)
        grad_rows = inv_ref[span, :1] * (scaled - first - unit * second)
        own = grad_ref[i * BLOCK : (i + 1) * BLOCK].astype(F32)
        grad_rows = jnp.concatenate([grad_rows[:TAIL], grad_rows[TAIL:] + own], axis=0)
        grad_context_ref[span] = dot(
            grad_rows.astype(BF16), w_out_ref[...], ((1,), (1,))
        ).astype(BF16)

    for i in range(2):
        for pair in range(PAIRS):
            columns = slice(pair * LANES, (pair + 1) * LANES)
            value_columns = slice(QUERY + pair * LANES, QUERY + (pair + 1) * LANES)
            span = slice(i * SPAN, (i + 1) * SPAN)
            rows = slice(i * ROWS, (i + 1) * ROWS)
            grads = stack_heads(grad_context_ref[rows, columns])
            q = stack_heads(query_ref[rows, columns])
            context = context_ref[rows, columns].astype(F32)
            context = jnp.concatenate([context, context], axis=0)
            delta = jnp.sum(grads.astype(F32) * context, axis=-1, keepdims=True)
            grad_probs = dot(grads, kv_ref[span, value_columns], ((1,), (1,)))
            grad_raw = (slope_ref[i * PAIRS + pair] * (grad_probs - delta)).astype(BF16)
            term_ref[span, columns] = dot(grad_raw, q, ((0,), (0,))).astype(BF16)
            term_ref[span, value_columns] = dot(
                probs_ref[i * PAIRS + pair], grads, ((0,), (0,))
            ).astype(BF16)

    half = WIDTH // NZ_LO
    for x in range(NX):
        for z_lo in range(NZ_LO):
            start = z_lo * half + x * LANES
            part = dot(
                normed_ref[:, start : start + LANES], term_ref[...], ((0,), (0,))
            )
            for t in range(TIME):
                parts_ref[t % 2, x, t // 2, z_lo] = part[
                    :, t * LANES : (t + 1) * LANES
                ].astype(BF16)


def local_pass(
    gathered,
    out_grad,
    gain1,
    w_query,
    w_kv,
    w_out,
    gain2,
    taps,
    bias,
    lengths,
    slots,
    counts,
):
    vmem = pl.BlockSpec(memory_space=pltpu.VMEM)
    smem = pl.BlockSpec(memory_space=pltpu.SMEM)
    both = 2 * ROWS
    return pl.pallas_call(
        local_kernel,
        out_shape=(
            jax.ShapeDtypeStruct((2 * BLOCK, WIDTH), BF16),
            jax.ShapeDtypeStruct((2, NX, NZ_HI, NZ_LO, LANES, LANES), BF16),
        ),
        in_specs=[smem] * 3 + [vmem] * 9,
        out_specs=(vmem, vmem),
        scratch_shapes=[
            pltpu.VMEM((2 * SPAN, WIDTH), BF16),
            pltpu.VMEM((2 * SPAN, KEYVAL), BF16),
            pltpu.VMEM((both, QUERY), BF16),
            pltpu.VMEM((both, WIDTH), F32),
            pltpu.VMEM((2 * PAIRS, both, SPAN), BF16),
            pltpu.VMEM((2 * PAIRS, both, SPAN), F32),
            pltpu.VMEM((both, QUERY), BF16),
            pltpu.VMEM((both, WIDTH), F32),
            pltpu.VMEM((both, WIDTH), F32),
            pltpu.VMEM((both, LANES), F32),
            pltpu.VMEM((both, WIDTH), F32),
            pltpu.VMEM((8, LANES), F32),
            pltpu.VMEM((both, WIDTH), F32),
            pltpu.VMEM((both, QUERY), BF16),
            pltpu.VMEM((2 * SPAN, KEYVAL), BF16),
        ],
        compiler_params=pltpu.CompilerParams(vmem_limit_bytes=40 << 20),
        name="local_pass",
    )(
        lengths,
        slots,
        counts,
        gathered,
        out_grad,
        gain1,
        w_query,
        w_kv,
        w_out,
        gain2,
        taps,
        bias,
    )


def reduce_kernel(
    parts_ref,
    out_ref,
    pair_ref,
    mine_ref,
    far_up_ref,
    far_down_ref,
    left_ref,
    right_ref,
    plane_ref,
    plane_in_ref,
    line_ref,
    line_in_ref,
    send_sem,
    recv_sem,
):
    dp = lax.axis_index("dp")
    tm = lax.axis_index("tm")
    z_lo, x, y = dp // (NX * NY), (dp // NY) % NX, dp % NY
    z_hi, core = tm // 2, tm % 2
    sibling = z_hi * 2 + 1 - core

    def at(other_z_lo, other_x, other_y):
        return (other_z_lo * NX + other_x) * NY + other_y

    up, down = (x + 1) % NX, (x + NX - 1) % NX
    far = (x + 2) % NX
    dp_up, dp_down = at(z_lo, up, y), at(z_lo, down, y)
    plane = [(y + step) % NY for step in range(1, NY)]
    line = [
        ((z_hi + step // NZ_LO) % NZ_HI, (z_lo + step % NZ_LO) % NZ_LO)
        for step in range(1, NZ_HI * NZ_LO)
    ]
    greet(
        [(dp, sibling), (dp_up, tm), (dp_down, tm)]
        + [(at(z_lo, x, other), tm) for other in plane]
        + [(at(other_lo, x, y), other_hi * 2 + core) for other_hi, other_lo in line]
    )
    copies = []

    def put(src, dst, number, target_dp, target_tm):
        copy = send(
            src, dst, send_sem.at[number], recv_sem.at[number], target_dp, target_tm
        )
        copy.start()
        copies.append(copy)
        return copy

    order = [far, up, down, x]
    across = [
        put(parts_ref.at[1 - core, other], pair_ref.at[other], n, dp, sibling)
        for n, other in enumerate(order)
    ]

    def add_pair(other):
        return parts_ref[core, other].astype(F32) + pair_ref[other].astype(F32)

    half = NZ_HI // 2
    lower, upper = pl.ds(0, half), pl.ds(half, half)
    across[0].wait_recv()
    mine_ref[far] = add_pair(far).astype(BF16)
    first = put(mine_ref.at[far, lower], far_up_ref, 4, dp_up, tm)
    second = put(mine_ref.at[far, upper], far_down_ref, 5, dp_down, tm)
    across[1].wait_recv()
    mine_ref[up] = add_pair(up).astype(BF16)
    from_left = [put(mine_ref.at[up, upper], left_ref.at[upper], 6, dp_up, tm)]
    across[2].wait_recv()
    mine_ref[down] = add_pair(down).astype(BF16)
    from_right = [put(mine_ref.at[down, lower], right_ref.at[lower], 7, dp_down, tm)]
    first.wait_recv()
    mine_ref[up, lower] = (
        mine_ref[up, lower].astype(F32) + far_up_ref[...].astype(F32)
    ).astype(BF16)
    from_left.append(put(mine_ref.at[up, lower], left_ref.at[lower], 8, dp_up, tm))
    second.wait_recv()
    mine_ref[down, upper] = (
        mine_ref[down, upper].astype(F32) + far_down_ref[...].astype(F32)
    ).astype(BF16)
    from_right.append(
        put(mine_ref.at[down, upper], right_ref.at[upper], 9, dp_down, tm)
    )
    across[3].wait_recv()
    for copy in from_left + from_right:
        copy.wait_recv()
    total = add_pair(x) + left_ref[...].astype(F32) + right_ref[...].astype(F32)
    for other in range(NY):
        plane_ref[other] = total[:, :, other * 16 : (other + 1) * 16].astype(BF16)

    incoming = [
        put(
            plane_ref.at[other],
            plane_in_ref.at[n],
            10 + n,
            at(z_lo, x, other),
            tm,
        )
        for n, other in enumerate(plane)
    ]
    summed = plane_ref[y].astype(F32)
    for n, copy in enumerate(incoming):
        copy.wait_recv()
        summed = summed + plane_in_ref[n].astype(F32)
    line_ref[...] = summed

    incoming = [
        put(
            line_ref.at[other_hi, other_lo],
            line_in_ref.at[n],
            17 + n,
            at(other_lo, x, y),
            other_hi * 2 + core,
        )
        for n, (other_hi, other_lo) in enumerate(line)
    ]
    summed = line_ref[z_hi, z_lo]
    for n, copy in enumerate(incoming):
        copy.wait_recv()
        summed = summed + line_in_ref[n]
    out_ref[...] = summed
    for copy in copies:
        copy.wait_send()


def reduce_parts(parts):
    chunk = (NZ_HI, NZ_LO, LANES, LANES)
    half = (NZ_HI // 2, NZ_LO, LANES, LANES)
    piece = (NZ_HI, NZ_LO, 16, LANES)
    return pl.pallas_call(
        reduce_kernel,
        out_shape=jax.ShapeDtypeStruct((16, LANES), F32),
        in_specs=[pl.BlockSpec(memory_space=pltpu.VMEM)],
        out_specs=pl.BlockSpec(memory_space=pltpu.VMEM),
        scratch_shapes=[
            pltpu.VMEM((NX, *chunk), BF16),
            pltpu.VMEM((NX, *chunk), BF16),
            pltpu.VMEM(half, BF16),
            pltpu.VMEM(half, BF16),
            pltpu.VMEM(chunk, BF16),
            pltpu.VMEM(chunk, BF16),
            pltpu.VMEM((NY, *piece), BF16),
            pltpu.VMEM((NY - 1, *piece), BF16),
            pltpu.VMEM(piece, F32),
            pltpu.VMEM((NZ_HI * NZ_LO - 1, 16, LANES), F32),
            pltpu.SemaphoreType.DMA((24,)),
            pltpu.SemaphoreType.DMA((24,)),
        ],
        compiler_params=pltpu.CompilerParams(
            collective_id=1, has_side_effects=True, vmem_limit_bytes=32 << 20
        ),
        name="reduce_parts",
    )(parts)


def on_device(
    frames,
    out_grad,
    norm1_gain,
    w_query,
    w_kv,
    w_out,
    norm2_gain,
    conv_kernel,
    conv_bias,
    utt_blocks,
    block_slot,
    left_count,
):
    gathered = gather_frames(frames)
    layer_out, parts = local_pass(
        gathered,
        out_grad,
        norm1_gain.reshape(1, WIDTH),
        w_query,
        w_kv,
        w_out,
        norm2_gain.reshape(1, WIDTH),
        conv_kernel,
        conv_bias.reshape(1, WIDTH),
        utt_blocks,
        block_slot,
        left_count,
    )
    return layer_out, reduce_parts(parts)


def solution(mesh):
    return jax.shard_map(
        on_device,
        mesh=mesh,
        in_specs=(
            P(("dp", "tm"), None),
            P(("dp", "tm"), None),
            P(),
            P(),
            P(),
            P(),
            P(),
            P(),
            P(),
            P("dp", None),
            P("dp", None),
            P("dp", None),
        ),
        out_specs=(P(("dp", "tm"), None), P("dp", "tm")),
        check_vma=False,
    )
```

```python
import jax
import jax.numpy as jnp
from jax import lax
from jax.experimental import pallas as pl
from jax.experimental.pallas import tpu as pltpu
from jax.sharding import PartitionSpec as P

HEADS = 8
HEAD = 64
PAIRS = HEADS // 2
TAPS = 31
BLOCK = 64
BLOCKS = 16
TIME = 8
UTTERANCES = 4
WIDTH = 1024
QUERY = 512
KEYVAL = 1024
LANES = 128
TAIL = 32
ROWS = TAIL + BLOCK
SPAN = 4 * BLOCK
NX, NY, NZ_LO, NZ_HI = 4, 8, 2, 4
PIECE = 16
EPSILON = 1e-05
SOFT_CAP = 4.0
MESH = pl.DeviceIdType.MESH
F32 = jnp.float32
BF16 = jnp.bfloat16


def unit_rows(rows):
    row_mean = jnp.mean(rows, axis=-1, keepdims=True)
    centred = rows - row_mean
    inv = lax.rsqrt(jnp.mean(centred * centred, axis=-1, keepdims=True) + EPSILON)
    return centred * inv, inv


def dot(a, b, dims):
    return lax.dot_general(a, b, (dims, ((), ())), preferred_element_type=F32)


def stack_heads(pair_rows):
    lane = lax.broadcasted_iota(jnp.int32, pair_rows.shape, 1)
    zero = jnp.zeros((), pair_rows.dtype)
    return jnp.concatenate(
        [
            jnp.where(lane < HEAD, pair_rows, zero),
            jnp.where(lane >= HEAD, pair_rows, zero),
        ],
        axis=0,
    )


def layer_kernel(
    lengths_ref,
    slots_ref,
    counts_ref,
    frames_hbm,
    grad_hbm,
    gain1_hbm,
    w_query_hbm,
    w_kv_hbm,
    w_out_hbm,
    gain2_hbm,
    taps_hbm,
    bias_hbm,
    out_hbm,
    share_ref,
    grad_ref,
    gain1_ref,
    w_query_ref,
    w_kv_ref,
    w_out_ref,
    gain2_ref,
    taps_ref,
    bias_ref,
    gath_ref,
    normed_ref,
    query_ref,
    kv_ref,
    probs_ref,
    slope_ref,
    context_ref,
    hidden_ref,
    unit_ref,
    inv_ref,
    conv_ref,
    back_ref,
    grad_context_ref,
    term_ref,
    out_ref,
    parts_ref,
    pair_ref,
    mine_ref,
    far_up_ref,
    far_down_ref,
    left_ref,
    right_ref,
    plane_ref,
    plane_in_ref,
    line_ref,
    line_in_ref,
    load_sem,
    send_sem,
    slot_sem,
    recv_sem,
):
    dp = lax.axis_index("dp")
    tm = lax.axis_index("tm")
    z_lo, x, y = dp // (NX * NY), (dp // NY) % NX, dp % NY
    z_hi, core = tm // 2, tm % 2
    sibling = z_hi * 2 + 1 - core
    above = ((z_hi + 1) % NZ_HI) * 2 + core
    below = ((z_hi + NZ_HI - 1) % NZ_HI) * 2 + core
    beyond = ((z_hi + 2) % NZ_HI) * 2 + core

    def at(other_z_lo, other_x, other_y):
        return (other_z_lo * NX + other_x) * NY + other_y

    up, down, far = (x + 1) % NX, (x + NX - 1) % NX, (x + 2) % NX
    dp_up, dp_down = at(z_lo, up, y), at(z_lo, down, y)
    plane = [at(z_lo, x, (y + step) % NY) for step in range(1, NY)]

    def line(turn, flip):
        return (
            at((z_lo + flip) % NZ_LO, x, y),
            ((z_hi + turn) % NZ_HI) * 2 + core,
        )

    loads = [
        pltpu.make_async_copy(src, dst, load_sem.at[n])
        for n, (src, dst) in enumerate(
            (
                (frames_hbm.at[pl.ds(0, BLOCK)], gath_ref.at[2 * tm]),
                (frames_hbm.at[pl.ds(BLOCK, BLOCK)], gath_ref.at[2 * tm + 1]),
                (gain1_hbm, gain1_ref),
                (w_query_hbm, w_query_ref),
                (w_kv_hbm, w_kv_ref),
                (w_out_hbm, w_out_ref),
                (gain2_hbm, gain2_ref),
                (taps_hbm, taps_ref),
                (bias_hbm, bias_ref),
                (grad_hbm, grad_ref),
            )
        )
    ]
    for copy in loads:
        copy.start()

    partners = [(dp, sibling), (dp_up, tm), (dp_down, tm)]
    partners += [(other, tm) for other in plane]
    partners += [
        line(turn, flip)
        for turn in range(NZ_HI)
        for flip in range(NZ_LO)
        if turn or flip
    ]
    barrier = pltpu.get_barrier_semaphore()
    for partner in partners:
        pl.semaphore_signal(barrier, inc=1, device_id=partner, device_id_type=MESH)
    pl.semaphore_wait(barrier, len(partners))

    sent = []

    def put(src, dst, arrival, target):
        copy = pltpu.make_async_remote_copy(
            src_ref=src,
            dst_ref=dst,
            send_sem=send_sem.at[len(sent)],
            recv_sem=arrival,
            device_id=target,
            device_id_type=MESH,
        )
        copy.start()
        sent.append(copy)
        return copy

    def pass_on(src, slot, target):
        put(src, gath_ref.at[slot], slot_sem.at[slot], (dp, target))

    def landed(slot):
        pltpu.make_async_remote_copy(
            src_ref=gath_ref.at[slot],
            dst_ref=gath_ref.at[slot],
            send_sem=send_sem.at[0],
            recv_sem=slot_sem.at[slot],
            device_id=(dp, sibling),
            device_id_type=MESH,
        ).wait_recv()

    own = [frames_hbm.at[pl.ds(b * BLOCK, BLOCK)] for b in range(2)]
    pass_on(own[0], 2 * tm, above)
    pass_on(own[1], 2 * tm + 1, below)
    pass_on(own[1], 2 * tm + 1, above)
    pass_on(own[0], 2 * tm, below)
    pass_on(own[0], 2 * tm, sibling)
    pass_on(own[1], 2 * tm + 1, sibling)

    def project(source):
        rows = gath_ref[pl.ds(2 * source, 2)].reshape(2 * BLOCK, WIDTH).astype(F32)
        unit, _ = unit_rows(rows)
        normed = (unit * gain1_ref[...]).astype(BF16)
        normed_ref[pl.ds(2 * source, 2)] = normed.reshape(2, BLOCK, WIDTH)
        queries = dot(normed, w_query_ref[...], ((1,), (0,))).astype(BF16)
        query_ref[pl.ds(2 * source, 2)] = queries.reshape(2, BLOCK, QUERY)
        keys_values = dot(normed, w_kv_ref[...], ((1,), (0,))).astype(BF16)
        kv_ref[pl.ds(2 * source, 2)] = keys_values.reshape(2, BLOCK, KEYVAL)

    def other_core(source):
        return source + 1 - 2 * core

    for copy in loads[:5]:
        copy.wait()
    project(tm)
    landed(2 * sibling)
    landed(2 * sibling + 1)
    project(sibling)
    landed(2 * below)
    pass_on(gath_ref.at[2 * below], 2 * below, above)
    pass_on(gath_ref.at[2 * below], 2 * below, sibling)
    landed(2 * above + 1)
    pass_on(gath_ref.at[2 * above + 1], 2 * above + 1, below)
    pass_on(gath_ref.at[2 * above + 1], 2 * above + 1, sibling)
    landed(2 * below + 1)
    pass_on(gath_ref.at[2 * below + 1], 2 * below + 1, sibling)
    landed(2 * above)
    pass_on(gath_ref.at[2 * above], 2 * above, sibling)
    project(below)
    project(above)
    for source in (other_core(below), other_core(above)):
        landed(2 * source)
        landed(2 * source + 1)
        project(source)
    landed(2 * beyond)
    pass_on(gath_ref.at[2 * beyond], 2 * beyond, sibling)
    landed(2 * beyond + 1)
    pass_on(gath_ref.at[2 * beyond + 1], 2 * beyond + 1, sibling)
    project(beyond)
    landed(2 * other_core(beyond))
    landed(2 * other_core(beyond) + 1)
    project(other_core(beyond))
    for copy in loads[5:]:
        copy.wait()

    def position(block):
        end, start = jnp.int32(0), jnp.int32(0)
        for u in range(UTTERANCES):
            length = lengths_ref[0, u]
            end = end + length
            start = start + jnp.where(block >= end, length, 0)
        return block - start

    blocks = []
    for i in range(2):
        block = jnp.int32(0)
        for b in range(BLOCKS):
            block = jnp.where(slots_ref[0, b] == 2 * tm + i, b, block)
        before = jnp.maximum(block - 1, 0)
        here, there = position(block), position(before)
        reach = jnp.minimum(counts_ref[0, block], here)
        reach_before = jnp.minimum(counts_ref[0, before], there)
        window = [slots_ref[0, jnp.maximum(block - 3 + lane, 0)] for lane in range(4)]
        blocks.append((reach, reach_before, here >= 1, window))

    def tail_and_own(ref, i, lanes):
        _, _, _, window = blocks[i]
        return jnp.concatenate(
            [ref[window[2], BLOCK - TAIL :, lanes], ref[window[3], :, lanes]], axis=0
        )

    def spanned(ref, i, lanes):
        return jnp.concatenate(
            [ref[slot, :, lanes] for slot in blocks[i][3]], axis=0
        )

    key_lane = lax.broadcasted_iota(jnp.int32, (ROWS, SPAN), 1) // BLOCK
    row = lax.broadcasted_iota(jnp.int32, (ROWS, SPAN), 0)
    lane = lax.broadcasted_iota(jnp.int32, (ROWS, LANES), 1)
    for i in range(2):
        reach, reach_before, _, _ = blocks[i]
        last = jnp.where(row < TAIL, 2, 3)
        first = last - jnp.where(row < TAIL, reach_before, reach)
        allowed = jnp.where((key_lane >= first) & (key_lane <= last), 1.0, 0.0)
        allowed = jnp.concatenate([allowed, allowed], axis=0)
        for pair in range(PAIRS):
            columns = slice(pair * LANES, (pair + 1) * LANES)
            value_columns = slice(QUERY + pair * LANES, QUERY + (pair + 1) * LANES)
            q = stack_heads(tail_and_own(query_ref, i, columns))
            raw = dot(q, spanned(kv_ref, i, columns), ((1,), (1,)))
            bent = jnp.tanh(raw * (1.0 / (SOFT_CAP * 8.0)))
            exped = jnp.exp(SOFT_CAP * bent) * allowed
            probs = exped * (1.0 / jnp.sum(exped, axis=-1, keepdims=True))
            probs_b = probs.astype(BF16)
            probs_ref[i * PAIRS + pair] = probs_b
            slope_ref[i * PAIRS + pair] = probs * (1.0 - bent * bent) * 0.125
            both = dot(probs_b, spanned(kv_ref, i, value_columns), ((1,), (0,)))
            context_ref[i * ROWS : (i + 1) * ROWS, columns] = jnp.where(
                lane < HEAD, both[:ROWS], both[ROWS:]
            ).astype(BF16)

    gain2 = gain2_ref[...]
    whole = slice(0, WIDTH)
    projected = dot(context_ref[...], w_out_ref[...], ((1,), (0,)))
    for i in range(2):
        span = slice(i * ROWS, (i + 1) * ROWS)
        hidden = tail_and_own(gath_ref, i, whole).astype(F32) + projected[span]
        hidden_ref[span] = hidden
        unit, inv = unit_rows(hidden)
        unit_ref[span] = unit
        inv_ref[span] = jnp.broadcast_to(inv, (ROWS, LANES))
        conv_in = (unit * gain2).astype(BF16).astype(F32)
        keep = jnp.where(blocks[i][2], 1.0, 0.0)
        conv_ref[i * ROWS : i * ROWS + TAIL] = conv_in[:TAIL] * keep
        conv_ref[i * ROWS + TAIL : (i + 1) * ROWS] = conv_in[TAIL:]

    for i in range(2):
        keep = jnp.where(blocks[i][2], 1.0, 0.0)

        def strip_pass(strip, carry):
            lanes = pl.ds(pl.multiple_of(strip * LANES, LANES), LANES)
            ext = conv_ref[i * ROWS : (i + 1) * ROWS, lanes]
            mixed = jnp.broadcast_to(bias_ref[:, lanes], (BLOCK, LANES))
            for shift in range(8):
                turned = ext if shift == 0 else pltpu.roll(ext, ROWS - shift, axis=0)
                for base in range(0, 40, 8):
                    tap = base + shift - 2
                    if 0 <= tap < TAPS:
                        mixed = (
                            mixed
                            + taps_ref[tap : tap + 1, lanes]
                            * turned[base : base + BLOCK]
                        )
            gate = 1.0 / (1.0 + jnp.exp(-mixed))
            hidden = hidden_ref[i * ROWS + TAIL : (i + 1) * ROWS, lanes]
            out_ref[i * BLOCK : (i + 1) * BLOCK, lanes] = (
                hidden + mixed * gate
            ).astype(BF16)
            out_grad = grad_ref[i * BLOCK : (i + 1) * BLOCK, lanes].astype(F32)
            grad_mixed = out_grad * gate * (1.0 + mixed * (1.0 - gate))
            zeros = jnp.zeros((TAIL, LANES), F32)
            padded = jnp.concatenate([zeros, grad_mixed, zeros], axis=0)
            total = jnp.zeros((ROWS, LANES), F32)
            for shift in range(8):
                turned = (
                    padded
                    if shift == 0
                    else pltpu.roll(padded, ROWS + TAIL - shift, axis=0)
                )
                for base in range(0, 32, 8):
                    tap = TAPS - 1 - base - shift
                    if 0 <= tap < TAPS:
                        total = (
                            total
                            + taps_ref[tap : tap + 1, lanes]
                            * turned[base : base + ROWS]
                        )
            back_ref[i * ROWS : i * ROWS + TAIL, lanes] = total[:TAIL] * keep
            back_ref[i * ROWS + TAIL : (i + 1) * ROWS, lanes] = total[TAIL:]
            return carry

        lax.fori_loop(0, WIDTH // LANES, strip_pass, 0)
    store = pltpu.make_async_copy(out_ref, out_hbm, load_sem.at[len(loads)])
    store.start()

    for i in range(2):
        span = slice(i * ROWS, (i + 1) * ROWS)
        scaled = back_ref[span] * gain2
        unit = unit_ref[span]
        first = jnp.mean(scaled, axis=-1, keepdims=True)
        second = jnp.mean(scaled * unit, axis=-1, keepdims=True)
        grad_rows = inv_ref[span, :1] * (scaled - first - unit * second)
        own_rows = grad_ref[i * BLOCK : (i + 1) * BLOCK].astype(F32)
        grad_rows = jnp.concatenate(
            [grad_rows[:TAIL], grad_rows[TAIL:] + own_rows], axis=0
        )
        grad_context_ref[span] = dot(
            grad_rows.astype(BF16), w_out_ref[...], ((1,), (1,))
        ).astype(BF16)

    for i in range(2):
        for pair in range(PAIRS):
            columns = slice(pair * LANES, (pair + 1) * LANES)
            value_columns = slice(QUERY + pair * LANES, QUERY + (pair + 1) * LANES)
            span = slice(i * SPAN, (i + 1) * SPAN)
            rows = slice(i * ROWS, (i + 1) * ROWS)
            grads = stack_heads(grad_context_ref[rows, columns])
            q = stack_heads(tail_and_own(query_ref, i, columns))
            context = context_ref[rows, columns].astype(F32)
            context = jnp.concatenate([context, context], axis=0)
            delta = jnp.sum(grads.astype(F32) * context, axis=-1, keepdims=True)
            grad_probs = dot(grads, spanned(kv_ref, i, value_columns), ((1,), (1,)))
            grad_raw = (slope_ref[i * PAIRS + pair] * (grad_probs - delta)).astype(BF16)
            term_ref[pair, span] = dot(grad_raw, q, ((0,), (0,))).astype(BF16)
            term_ref[PAIRS + pair, span] = dot(
                probs_ref[i * PAIRS + pair], grads, ((0,), (0,))
            ).astype(BF16)

    def product(other, parity):
        left = jnp.concatenate(
            [
                jnp.concatenate(
                    [
                        spanned(
                            normed_ref,
                            i,
                            pl.ds(
                                pl.multiple_of(
                                    (half * NX + other) * LANES, LANES
                                ),
                                LANES,
                            ),
                        )
                        for i in range(2)
                    ],
                    axis=0,
                )
                for half in range(NZ_LO)
            ],
            axis=1,
        )
        right = jnp.concatenate(
            [
                term_ref[((z_hi + turn) % NZ_HI) * 2 + parity]
                for turn in range(NZ_HI)
            ],
            axis=1,
        )
        return dot(left, right, ((0,), (0,)))

    def tile(rows, turn, half):
        return rows[
            half * LANES : (half + 1) * LANES, turn * LANES : (turn + 1) * LANES
        ]

    order = [far, up, down, x]
    across = []
    for n, other in enumerate(order):
        rows = product(other, 1 - core)
        for turn in range(NZ_HI):
            for half in range(NZ_LO):
                parts_ref[n, turn, half] = tile(rows, turn, half).astype(BF16)
        across.append(
            put(parts_ref.at[n], pair_ref.at[n], recv_sem.at[n], (dp, sibling))
        )

    def add_pair(n):
        rows = product(order[n], core)
        across[n].wait_recv()
        for turn in range(NZ_HI):
            for half in range(NZ_LO):
                mine_ref[n, turn, half] = (
                    tile(rows, turn, half) + pair_ref[n, turn, half].astype(F32)
                ).astype(BF16)

    add_pair(0)
    to_up = [
        put(mine_ref.at[0, n], far_up_ref.at[n], recv_sem.at[4 + n], (dp_up, tm))
        for n in range(2)
    ]
    to_down = [
        put(
            mine_ref.at[0, 2 + n], far_down_ref.at[n], recv_sem.at[6 + n], (dp_down, tm)
        )
        for n in range(2)
    ]
    add_pair(1)
    lower, upper = pl.ds(0, 2), pl.ds(2, 2)
    from_left = put(
        mine_ref.at[1, upper], left_ref.at[upper], recv_sem.at[8], (dp_up, tm)
    )
    add_pair(2)
    from_right = put(
        mine_ref.at[2, lower], right_ref.at[lower], recv_sem.at[9], (dp_down, tm)
    )
    late_left, late_right = [], []
    for n in range(2):
        to_up[n].wait_recv()
        mine_ref[1, n] = (
            mine_ref[1, n].astype(F32) + far_up_ref[n].astype(F32)
        ).astype(BF16)
        late_left.append(
            put(mine_ref.at[1, n], left_ref.at[n], recv_sem.at[10 + n], (dp_up, tm))
        )
        to_down[n].wait_recv()
        mine_ref[2, 2 + n] = (
            mine_ref[2, 2 + n].astype(F32) + far_down_ref[n].astype(F32)
        ).astype(BF16)
        late_right.append(
            put(
                mine_ref.at[2, 2 + n],
                right_ref.at[2 + n],
                recv_sem.at[12 + n],
                (dp_down, tm),
            )
        )
    add_pair(3)
    from_left.wait_recv()
    from_right.wait_recv()
    arrivals = 14
    in_plane = []
    for n in range(2):
        late_left[n].wait_recv()
        late_right[n].wait_recv()
        for m in range(2):
            turn = 2 * m + n
            total = (
                mine_ref[3, turn].astype(F32)
                + left_ref[turn].astype(F32)
                + right_ref[turn].astype(F32)
            ).astype(BF16)
            for other in range(NY):
                plane_ref[n, other, m] = total[
                    :, other * PIECE : (other + 1) * PIECE
                ]
        in_plane.append(
            [
                put(
                    plane_ref.at[n, (y + step) % NY],
                    plane_in_ref.at[n, step - 1],
                    recv_sem.at[arrivals + n * (NY - 1) + step - 1],
                    (plane[step - 1], tm),
                )
                for step in range(1, NY)
            ]
        )
    arrivals += 2 * (NY - 1)
    in_line = []
    for n in range(2):
        summed = plane_ref[n, y].astype(F32)
        for step in range(1, NY):
            in_plane[n][step - 1].wait_recv()
            summed = summed + plane_in_ref[n, step - 1].astype(F32)
        for m in range(2):
            turn = 2 * m + n
            line_ref[turn] = summed[m]
            for flip in range(NZ_LO):
                number = 2 * turn + flip - 1
                if number >= 0:
                    in_line.append(
                        put(
                            line_ref.at[turn, (z_lo + flip) % NZ_LO],
                            line_in_ref.at[number],
                            recv_sem.at[arrivals + number],
                            line(turn, flip),
                        )
                    )
    for copy in in_line:
        copy.wait_recv()
    summed = line_ref[0, z_lo]
    for number in range(NZ_HI * NZ_LO - 1):
        summed = summed + line_in_ref[number]
    share_ref[...] = summed
    store.wait()
    for copy in sent:
        copy.wait_send()


def forward(
    frames,
    out_grad,
    norm1_gain,
    w_query,
    w_kv,
    w_out,
    norm2_gain,
    conv_kernel,
    conv_bias,
    utt_blocks,
    block_slot,
    left_count,
):
    smem = pl.BlockSpec(memory_space=pltpu.SMEM)
    hbm = pl.BlockSpec(memory_space=pl.ANY)
    both = 2 * ROWS
    chunk = (NZ_HI, NZ_LO, LANES, LANES)
    halves = (2, NZ_LO, LANES, LANES)
    piece = (2, NZ_LO, PIECE, LANES)
    vmem = pltpu.VMEM
    return pl.pallas_call(
        layer_kernel,
        out_shape=(
            jax.ShapeDtypeStruct((2 * BLOCK, WIDTH), BF16),
            jax.ShapeDtypeStruct((PIECE, LANES), F32),
        ),
        in_specs=[smem] * 3 + [hbm] * 9,
        out_specs=(hbm, pl.BlockSpec(memory_space=pltpu.VMEM)),
        scratch_shapes=[
            vmem((2 * BLOCK, WIDTH), BF16),
            vmem((1, WIDTH), F32),
            vmem((WIDTH, QUERY), BF16),
            vmem((WIDTH, KEYVAL), BF16),
            vmem((QUERY, WIDTH), BF16),
            vmem((1, WIDTH), F32),
            vmem((TAPS, WIDTH), F32),
            vmem((1, WIDTH), F32),
            vmem((BLOCKS, BLOCK, WIDTH), BF16),
            vmem((BLOCKS, BLOCK, WIDTH), BF16),
            vmem((BLOCKS, BLOCK, QUERY), BF16),
            vmem((BLOCKS, BLOCK, KEYVAL), BF16),
            vmem((2 * PAIRS, both, SPAN), BF16),
            vmem((2 * PAIRS, both, SPAN), F32),
            vmem((both, QUERY), BF16),
            vmem((both, WIDTH), F32),
            vmem((both, WIDTH), F32),
            vmem((both, LANES), F32),
            vmem((both, WIDTH), F32),
            vmem((both, WIDTH), F32),
            vmem((both, QUERY), BF16),
            vmem((TIME, 2 * SPAN, LANES), BF16),
            vmem((2 * BLOCK, WIDTH), BF16),
            vmem((NX, *chunk), BF16),
            vmem((NX, *chunk), BF16),
            vmem((NX, *chunk), BF16),
            vmem(halves, BF16),
            vmem(halves, BF16),
            vmem(chunk, BF16),
            vmem(chunk, BF16),
            vmem((2, NY, *piece), BF16),
            vmem((2, NY - 1, *piece), BF16),
            vmem((NZ_HI, NZ_LO, PIECE, LANES), F32),
            vmem((NZ_HI * NZ_LO - 1, PIECE, LANES), F32),
            pltpu.SemaphoreType.DMA((11,)),
            pltpu.SemaphoreType.DMA((49,)),
            pltpu.SemaphoreType.DMA((BLOCKS,)),
            pltpu.SemaphoreType.DMA((35,)),
        ],
        compiler_params=pltpu.CompilerParams(
            collective_id=0, has_side_effects=True, vmem_limit_bytes=56 << 20
        ),
        name="layer",
    )(
        utt_blocks,
        block_slot,
        left_count,
        frames,
        out_grad,
        norm1_gain.reshape(1, WIDTH),
        w_query,
        w_kv,
        w_out,
        norm2_gain.reshape(1, WIDTH),
        conv_kernel,
        conv_bias.reshape(1, WIDTH),
    )


def solution(mesh):
    return jax.shard_map(
        forward,
        mesh=mesh,
        in_specs=(
            P(("dp", "tm"), None),
            P(("dp", "tm"), None),
            P(),
            P(),
            P(),
            P(),
            P(),
            P(),
            P(),
            P("dp", None),
            P("dp", None),
            P("dp", None),
        ),
        out_specs=(P(("dp", "tm"), None), P("dp", "tm")),
        check_vma=False,
    )
```

```python
import jax
import jax.numpy as jnp
from jax import lax
from jax.experimental import pallas as pl
from jax.experimental.pallas import tpu as pltpu
from jax.sharding import PartitionSpec as P

HEADS = 8
HEAD = 64
PAIRS = HEADS // 2
TAPS = 31
BLOCK = 64
BLOCKS = 16
TIME = 8
UTTERANCES = 4
WIDTH = 1024
QUERY = 512
KEYVAL = 1024
LANES = 128
TAIL = 32
ROWS = TAIL + BLOCK
SPAN = 4 * BLOCK
NX, NY, NZ_LO, NZ_HI = 4, 8, 2, 4
PIECE = 16
EPSILON = 1e-05
SOFT_CAP = 4.0
MESH = pl.DeviceIdType.MESH
F32 = jnp.float32
BF16 = jnp.bfloat16


def unit_rows(rows):
    row_mean = jnp.mean(rows, axis=-1, keepdims=True)
    centred = rows - row_mean
    inv = lax.rsqrt(jnp.mean(centred * centred, axis=-1, keepdims=True) + EPSILON)
    return centred * inv, inv


def dot(a, b, dims):
    return lax.dot_general(a, b, (dims, ((), ())), preferred_element_type=F32)


def stack_heads(pair_rows):
    lane = lax.broadcasted_iota(jnp.int32, pair_rows.shape, 1)
    zero = jnp.zeros((), pair_rows.dtype)
    return jnp.concatenate(
        [
            jnp.where(lane < HEAD, pair_rows, zero),
            jnp.where(lane >= HEAD, pair_rows, zero),
        ],
        axis=0,
    )


def layer_kernel(
    lengths_hbm,
    slots_hbm,
    counts_hbm,
    frames_hbm,
    grad_hbm,
    gain1_hbm,
    w_query_hbm,
    w_kv_hbm,
    w_out_hbm,
    gain2_hbm,
    taps_hbm,
    bias_hbm,
    out_ref,
    share_ref,
    lengths_ref,
    slots_ref,
    counts_ref,
    grad_ref,
    gain1_ref,
    w_query_ref,
    w_kv_ref,
    w_out_ref,
    gain2_ref,
    taps_ref,
    bias_ref,
    gath_ref,
    normed_ref,
    query_ref,
    kv_ref,
    probs_ref,
    slope_ref,
    context_ref,
    hidden_ref,
    unit_ref,
    inv_ref,
    conv_ref,
    back_ref,
    grad_context_ref,
    term_ref,
    turned_ref,
    flipped_ref,
    parts_ref,
    pair_ref,
    mine_ref,
    far_up_ref,
    far_down_ref,
    left_ref,
    right_ref,
    plane_ref,
    plane_in_ref,
    line_ref,
    line_in_ref,
    load_sem,
    send_sem,
    slot_sem,
    recv_sem,
):
    dp = lax.axis_index("dp")
    tm = lax.axis_index("tm")
    z_lo, x, y = dp // (NX * NY), (dp // NY) % NX, dp % NY
    z_hi, core = tm // 2, tm % 2
    sibling = z_hi * 2 + 1 - core
    above = ((z_hi + 1) % NZ_HI) * 2 + core
    below = ((z_hi + NZ_HI - 1) % NZ_HI) * 2 + core
    beyond = ((z_hi + 2) % NZ_HI) * 2 + core

    def at(other_z_lo, other_x, other_y):
        return (other_z_lo * NX + other_x) * NY + other_y

    up, down, far = (x + 1) % NX, (x + NX - 1) % NX, (x + 2) % NX
    dp_up, dp_down = at(z_lo, up, y), at(z_lo, down, y)
    plane = [at(z_lo, x, (y + step) % NY) for step in range(1, NY)]

    def line(turn, flip):
        return (
            at((z_lo + flip) % NZ_LO, x, y),
            ((z_hi + turn) % NZ_HI) * 2 + core,
        )

    loads = [
        pltpu.make_async_copy(src, dst, load_sem.at[n])
        for n, (src, dst) in enumerate(
            (
                (frames_hbm.at[pl.ds(0, BLOCK)], gath_ref.at[2 * tm]),
                (frames_hbm.at[pl.ds(BLOCK, BLOCK)], gath_ref.at[2 * tm + 1]),
                (gain1_hbm, gain1_ref),
                (w_query_hbm, w_query_ref),
                (w_kv_hbm, w_kv_ref),
                (w_out_hbm, w_out_ref),
                (gain2_hbm, gain2_ref),
                (taps_hbm, taps_ref),
                (bias_hbm, bias_ref),
                (grad_hbm, grad_ref),
                (lengths_hbm, lengths_ref),
                (slots_hbm, slots_ref),
                (counts_hbm, counts_ref),
            )
        )
    ]
    for copy in loads:
        copy.start()

    partners = [(dp, sibling), (dp_up, tm), (dp_down, tm)]
    partners += [(other, tm) for other in plane]
    partners += [
        line(turn, flip)
        for turn in range(NZ_HI)
        for flip in range(NZ_LO)
        if turn or flip
    ]
    barrier = pltpu.get_barrier_semaphore()
    for partner in partners:
        pl.semaphore_signal(barrier, inc=1, device_id=partner, device_id_type=MESH)
    pl.semaphore_wait(barrier, len(partners))

    sent = []

    def put(src, dst, arrival, target):
        copy = pltpu.make_async_remote_copy(
            src_ref=src,
            dst_ref=dst,
            send_sem=send_sem.at[len(sent)],
            recv_sem=arrival,
            device_id=target,
            device_id_type=MESH,
        )
        copy.start()
        sent.append(copy)
        return copy

    def pass_on(src, slot, target):
        put(src, gath_ref.at[slot], slot_sem.at[slot], (dp, target))

    def landed(slot):
        pltpu.make_async_remote_copy(
            src_ref=gath_ref.at[slot],
            dst_ref=gath_ref.at[slot],
            send_sem=send_sem.at[0],
            recv_sem=slot_sem.at[slot],
            device_id=(dp, sibling),
            device_id_type=MESH,
        ).wait_recv()

    own = [frames_hbm.at[pl.ds(b * BLOCK, BLOCK)] for b in range(2)]
    pass_on(own[0], 2 * tm, above)
    pass_on(own[1], 2 * tm + 1, below)
    pass_on(own[0], 2 * tm, sibling)
    pass_on(own[1], 2 * tm + 1, sibling)

    def project(source):
        rows = gath_ref[pl.ds(2 * source, 2)].reshape(2 * BLOCK, WIDTH).astype(F32)
        unit, _ = unit_rows(rows)
        normed = (unit * gain1_ref[...]).astype(BF16)
        normed_ref[pl.ds(2 * source, 2)] = normed.reshape(2, BLOCK, WIDTH)
        queries = dot(normed, w_query_ref[...], ((1,), (0,))).astype(BF16)
        query_ref[pl.ds(2 * source, 2)] = queries.reshape(2, BLOCK, QUERY)
        keys_values = dot(normed, w_kv_ref[...], ((1,), (0,))).astype(BF16)
        kv_ref[pl.ds(2 * source, 2)] = keys_values.reshape(2, BLOCK, KEYVAL)

    def other_core(source):
        return source + 1 - 2 * core

    for copy in loads[:5]:
        copy.wait()
    project(tm)
    leading = sent[:2]
    for copy in leading:
        copy.wait_send()
    pass_on(own[1], 2 * tm + 1, above)
    pass_on(own[0], 2 * tm, below)
    landed(2 * sibling)
    landed(2 * sibling + 1)
    project(sibling)
    landed(2 * below)
    pass_on(gath_ref.at[2 * below], 2 * below, above)
    pass_on(gath_ref.at[2 * below], 2 * below, sibling)
    landed(2 * above + 1)
    pass_on(gath_ref.at[2 * above + 1], 2 * above + 1, below)
    pass_on(gath_ref.at[2 * above + 1], 2 * above + 1, sibling)
    landed(2 * below + 1)
    pass_on(gath_ref.at[2 * below + 1], 2 * below + 1, sibling)
    landed(2 * above)
    pass_on(gath_ref.at[2 * above], 2 * above, sibling)
    project(below)
    project(above)
    for copy in loads[5:]:
        copy.wait()
    flipped_ref[...] = w_out_ref[...].T
    for source in (other_core(below), other_core(above)):
        landed(2 * source)
        landed(2 * source + 1)
        project(source)
    landed(2 * beyond)
    pass_on(gath_ref.at[2 * beyond], 2 * beyond, sibling)
    landed(2 * beyond + 1)
    pass_on(gath_ref.at[2 * beyond + 1], 2 * beyond + 1, sibling)
    project(beyond)
    landed(2 * other_core(beyond))
    landed(2 * other_core(beyond) + 1)
    project(other_core(beyond))

    def position(block):
        end, start = jnp.int32(0), jnp.int32(0)
        for u in range(UTTERANCES):
            length = lengths_ref[0, u]
            end = end + length
            start = start + jnp.where(block >= end, length, 0)
        return block - start

    blocks = []
    for i in range(2):
        block = jnp.int32(0)
        for b in range(BLOCKS):
            block = jnp.where(slots_ref[0, b] == 2 * tm + i, b, block)
        before = jnp.maximum(block - 1, 0)
        here, there = position(block), position(before)
        reach = jnp.minimum(counts_ref[0, block], here)
        reach_before = jnp.minimum(counts_ref[0, before], there)
        window = [slots_ref[0, jnp.maximum(block - 3 + lane, 0)] for lane in range(4)]
        blocks.append((reach, reach_before, here >= 1, window))

    def tail_and_own(ref, i, lanes):
        _, _, _, window = blocks[i]
        return jnp.concatenate(
            [ref[window[2], BLOCK - TAIL :, lanes], ref[window[3], :, lanes]], axis=0
        )

    def spanned(ref, i, lanes):
        return jnp.concatenate(
            [ref[slot, :, lanes] for slot in blocks[i][3]], axis=0
        )

    for i in range(2):
        for n in range(2):
            rows = jnp.concatenate(
                [normed_ref[slot] for slot in blocks[i][3][2 * n : 2 * n + 2]], axis=0
            )
            start = i * SPAN + n * LANES
            turned_ref[:, start : start + LANES] = rows.T

    key_lane = lax.broadcasted_iota(jnp.int32, (ROWS, SPAN), 1) // BLOCK
    row = lax.broadcasted_iota(jnp.int32, (ROWS, SPAN), 0)
    lane = lax.broadcasted_iota(jnp.int32, (ROWS, LANES), 1)
    allowed = []
    for i in range(2):
        reach, reach_before, _, _ = blocks[i]
        last = jnp.where(row < TAIL, 2, 3)
        first = last - jnp.where(row < TAIL, reach_before, reach)
        mask = jnp.where((key_lane >= first) & (key_lane <= last), 1.0, 0.0)
        allowed.append(jnp.concatenate([mask, mask], axis=0))

    def pair_columns(pair):
        return (
            slice(pair * LANES, (pair + 1) * LANES),
            slice(QUERY + pair * LANES, QUERY + (pair + 1) * LANES),
        )

    for pair in range(PAIRS):
        columns, value_columns = pair_columns(pair)
        both = range(2)
        q = [stack_heads(tail_and_own(query_ref, i, columns)) for i in both]
        raw = [dot(q[i], spanned(kv_ref, i, columns), ((1,), (1,))) for i in both]
        bent = [jnp.tanh(raw[i] * (1.0 / (SOFT_CAP * 8.0))) for i in both]
        exped = [jnp.exp(SOFT_CAP * bent[i]) * allowed[i] for i in both]
        scale = [1.0 / jnp.sum(exped[i], axis=-1, keepdims=True) for i in both]
        probs = [exped[i] * scale[i] for i in both]
        probs_b = [probs[i].astype(BF16) for i in both]
        heads = [
            dot(probs_b[i], spanned(kv_ref, i, value_columns), ((1,), (0,)))
            for i in both
        ]
        for i in both:
            probs_ref[i * PAIRS + pair] = probs_b[i]
            slope_ref[i * PAIRS + pair] = (
                probs[i] * (1.0 - bent[i] * bent[i]) * 0.125
            )
            context_ref[i * ROWS : (i + 1) * ROWS, columns] = jnp.where(
                lane < HEAD, heads[i][:ROWS], heads[i][ROWS:]
            ).astype(BF16)

    gain2 = gain2_ref[...]
    whole = slice(0, WIDTH)
    projected = dot(context_ref[...], w_out_ref[...], ((1,), (0,)))
    for i in range(2):
        span = slice(i * ROWS, (i + 1) * ROWS)
        hidden = tail_and_own(gath_ref, i, whole).astype(F32) + projected[span]
        hidden_ref[span] = hidden
        unit, inv = unit_rows(hidden)
        unit_ref[span] = unit
        inv_ref[span] = jnp.broadcast_to(inv, (ROWS, LANES))
        conv_in = (unit * gain2).astype(BF16).astype(F32)
        keep = jnp.where(blocks[i][2], 1.0, 0.0)
        conv_ref[i * ROWS : i * ROWS + TAIL] = conv_in[:TAIL] * keep
        conv_ref[i * ROWS + TAIL : (i + 1) * ROWS] = conv_in[TAIL:]

    for i in range(2):
        keep = jnp.where(blocks[i][2], 1.0, 0.0)

        def strip_pass(strip, carry):
            lanes = pl.ds(pl.multiple_of(strip * LANES, LANES), LANES)
            ext = conv_ref[i * ROWS : (i + 1) * ROWS, lanes]
            mixed = jnp.broadcast_to(bias_ref[:, lanes], (BLOCK, LANES))
            for shift in range(8):
                turned = ext if shift == 0 else pltpu.roll(ext, ROWS - shift, axis=0)
                for base in range(0, 40, 8):
                    tap = base + shift - 2
                    if 0 <= tap < TAPS:
                        mixed = (
                            mixed
                            + taps_ref[tap : tap + 1, lanes]
                            * turned[base : base + BLOCK]
                        )
            gate = 1.0 / (1.0 + jnp.exp(-mixed))
            hidden = hidden_ref[i * ROWS + TAIL : (i + 1) * ROWS, lanes]
            out_ref[i * BLOCK : (i + 1) * BLOCK, lanes] = (
                hidden + mixed * gate
            ).astype(BF16)
            out_grad = grad_ref[i * BLOCK : (i + 1) * BLOCK, lanes].astype(F32)
            grad_mixed = out_grad * gate * (1.0 + mixed * (1.0 - gate))
            zeros = jnp.zeros((8, LANES), F32)
            padded = jnp.concatenate([zeros, grad_mixed, zeros], axis=0)
            reached = [jnp.zeros((BLOCK + 8, LANES), F32) for _ in range(4)]
            for shift in range(8):
                turned = (
                    padded
                    if shift == 0
                    else pltpu.roll(padded, BLOCK + 16 - shift, axis=0)
                )[: BLOCK + 8]
                for base in range(4):
                    tap = TAPS - 1 - 8 * base - shift
                    if 0 <= tap < TAPS:
                        reached[base] = (
                            reached[base] + taps_ref[tap : tap + 1, lanes] * turned
                        )
            total = jnp.concatenate(
                [
                    sum(
                        reached[base][row - 24 + 8 * base : row - 16 + 8 * base]
                        for base in range(4)
                        if 0 <= row - 24 + 8 * base < BLOCK + 8
                    )
                    for row in range(0, ROWS, 8)
                ],
                axis=0,
            )
            back_ref[i * ROWS : i * ROWS + TAIL, lanes] = total[:TAIL] * keep
            back_ref[i * ROWS + TAIL : (i + 1) * ROWS, lanes] = total[TAIL:]
            return carry

        lax.fori_loop(0, WIDTH // LANES, strip_pass, 0)

    grad_rows = []
    for i in range(2):
        span = slice(i * ROWS, (i + 1) * ROWS)
        scaled = back_ref[span] * gain2
        unit = unit_ref[span]
        first = jnp.mean(scaled, axis=-1, keepdims=True)
        second = jnp.mean(scaled * unit, axis=-1, keepdims=True)
        grads = inv_ref[span, :1] * (scaled - first - unit * second)
        own_rows = grad_ref[i * BLOCK : (i + 1) * BLOCK].astype(F32)
        grad_rows += [grads[:TAIL].astype(BF16), (grads[TAIL:] + own_rows).astype(BF16)]
    grad_context_ref[...] = dot(
        jnp.concatenate(grad_rows, axis=0), flipped_ref[...], ((1,), (0,))
    ).astype(BF16)

    def pair_of(n, parity):
        return 2 * ((z_hi + n) % 2) + parity

    def differentiate(pair):
        columns = pl.ds(pl.multiple_of(pair * LANES, LANES), LANES)
        value_columns = pl.ds(pl.multiple_of(QUERY + pair * LANES, LANES), LANES)
        both = range(2)
        span = [slice(i * SPAN, (i + 1) * SPAN) for i in both]
        rows = [slice(i * ROWS, (i + 1) * ROWS) for i in both]
        grads = [stack_heads(grad_context_ref[rows[i], columns]) for i in both]
        grad_probs = [
            dot(grads[i], spanned(kv_ref, i, value_columns), ((1,), (1,)))
            for i in both
        ]
        value_terms = [
            dot(probs_ref[i * PAIRS + pair], grads[i], ((0,), (0,))) for i in both
        ]
        context = [context_ref[rows[i], columns].astype(F32) for i in both]
        delta = [
            jnp.sum(
                grads[i].astype(F32) * jnp.concatenate([context[i]] * 2, axis=0),
                axis=-1,
                keepdims=True,
            )
            for i in both
        ]
        grad_raw = [
            (slope_ref[i * PAIRS + pair] * (grad_probs[i] - delta[i])).astype(BF16)
            for i in both
        ]
        q = [stack_heads(tail_and_own(query_ref, i, columns)) for i in both]
        key_terms = [dot(grad_raw[i], q[i], ((0,), (0,))) for i in both]
        for i in both:
            term_ref[PAIRS + pair, span[i]] = value_terms[i].astype(BF16)
            term_ref[pair, span[i]] = key_terms[i].astype(BF16)

    def product(n, parity):
        right = jnp.concatenate(
            [
                term_ref[2 * ((z_hi + n + 2 * m) % NZ_HI) + parity]
                for m in range(2)
            ],
            axis=1,
        )
        return dot(turned_ref[...], right, ((1,), (0,)))

    tiles = [
        (other, m, half)
        for other in range(NX)
        for m in range(2)
        for half in range(NZ_LO)
    ]

    def tile(rows, other, m, half):
        start = (half * NX + other) * LANES
        return rows[start : start + LANES, m * LANES : (m + 1) * LANES]

    def share_pair(n):
        differentiate(pair_of(n, 1 - core))
        rows = product(n, 1 - core)
        for other, m, half in tiles:
            parts_ref[n, other, m, half] = tile(rows, other, m, half).astype(BF16)
        return put(parts_ref.at[n], pair_ref.at[n], recv_sem.at[n], (dp, sibling))

    def add_pair(n, shared):
        differentiate(pair_of(n, core))
        rows = product(n, core)
        shared.wait_recv()
        for other, m, half in tiles:
            mine_ref[n, other, m, half] = (
                tile(rows, other, m, half) + pair_ref[n, other, m, half].astype(F32)
            ).astype(BF16)

    def start_ring(n):
        return (
            put(mine_ref.at[n, far, 0], far_up_ref.at[n], recv_sem.at[2 + n], (dp_up, tm)),
            put(
                mine_ref.at[n, far, 1],
                far_down_ref.at[n],
                recv_sem.at[4 + n],
                (dp_down, tm),
            ),
            put(mine_ref.at[n, up, 1], left_ref.at[n, 1], recv_sem.at[6 + n], (dp_up, tm)),
            put(
                mine_ref.at[n, down, 0],
                right_ref.at[n, 0],
                recv_sem.at[8 + n],
                (dp_down, tm),
            ),
        )

    def end_ring(n, ring):
        ring[0].wait_recv()
        mine_ref[n, up, 0] = (
            mine_ref[n, up, 0].astype(F32) + far_up_ref[n].astype(F32)
        ).astype(BF16)
        left = put(
            mine_ref.at[n, up, 0], left_ref.at[n, 0], recv_sem.at[10 + n], (dp_up, tm)
        )
        ring[1].wait_recv()
        mine_ref[n, down, 1] = (
            mine_ref[n, down, 1].astype(F32) + far_down_ref[n].astype(F32)
        ).astype(BF16)
        right = put(
            mine_ref.at[n, down, 1],
            right_ref.at[n, 1],
            recv_sem.at[12 + n],
            (dp_down, tm),
        )
        return ring[2], ring[3], left, right

    shared = share_pair(0)
    add_pair(0, shared)
    ring_first = start_ring(0)
    shared = share_pair(1)
    add_pair(1, shared)
    ring_second = start_ring(1)
    rings = [end_ring(0, ring_first), end_ring(1, ring_second)]

    arrivals = 14
    in_plane = []
    for n in range(2):
        for copy in rings[n]:
            copy.wait_recv()
        for m in range(2):
            total = (
                mine_ref[n, x, m].astype(F32)
                + left_ref[n, m].astype(F32)
                + right_ref[n, m].astype(F32)
            ).astype(BF16)
            for other in range(NY):
                plane_ref[n, other, m] = total[
                    :, other * PIECE : (other + 1) * PIECE
                ]
        in_plane.append(
            [
                put(
                    plane_ref.at[n, (y + step) % NY],
                    plane_in_ref.at[n, step - 1],
                    recv_sem.at[arrivals + n * (NY - 1) + step - 1],
                    (plane[step - 1], tm),
                )
                for step in range(1, NY)
            ]
        )
    arrivals += 2 * (NY - 1)
    in_line = []
    for n in range(2):
        summed = plane_ref[n, y].astype(F32)
        for step in range(1, NY):
            in_plane[n][step - 1].wait_recv()
            summed = summed + plane_in_ref[n, step - 1].astype(F32)
        for m in range(2):
            turn = 2 * m + n
            line_ref[turn] = summed[m]
            for flip in range(NZ_LO):
                number = 2 * turn + flip - 1
                if number >= 0:
                    in_line.append(
                        put(
                            line_ref.at[turn, (z_lo + flip) % NZ_LO],
                            line_in_ref.at[number],
                            recv_sem.at[arrivals + number],
                            line(turn, flip),
                        )
                    )
    for copy in in_line:
        copy.wait_recv()
    summed = line_ref[0, z_lo]
    for number in range(NZ_HI * NZ_LO - 1):
        summed = summed + line_in_ref[number]
    share_ref[...] = summed
    for copy in sent[2:]:
        copy.wait_send()


def forward(
    frames,
    out_grad,
    norm1_gain,
    w_query,
    w_kv,
    w_out,
    norm2_gain,
    conv_kernel,
    conv_bias,
    utt_blocks,
    block_slot,
    left_count,
):
    hbm = pl.BlockSpec(memory_space=pltpu.MemorySpace.HBM)
    both = 2 * ROWS
    halves = (2, NZ_LO, LANES, LANES)
    piece = (2, NZ_LO, PIECE, LANES)
    vmem = pltpu.VMEM
    return pl.pallas_call(
        layer_kernel,
        out_shape=(
            jax.ShapeDtypeStruct((2 * BLOCK, WIDTH), BF16),
            jax.ShapeDtypeStruct((PIECE, LANES), F32),
        ),
        in_specs=[hbm] * 12,
        out_specs=(pl.BlockSpec(memory_space=pltpu.VMEM),) * 2,
        scratch_shapes=[
            pltpu.SMEM((1, UTTERANCES), jnp.int32),
            pltpu.SMEM((1, BLOCKS), jnp.int32),
            pltpu.SMEM((1, BLOCKS), jnp.int32),
            vmem((2 * BLOCK, WIDTH), BF16),
            vmem((1, WIDTH), F32),
            vmem((WIDTH, QUERY), BF16),
            vmem((WIDTH, KEYVAL), BF16),
            vmem((QUERY, WIDTH), BF16),
            vmem((1, WIDTH), F32),
            vmem((TAPS, WIDTH), F32),
            vmem((1, WIDTH), F32),
            vmem((BLOCKS, BLOCK, WIDTH), BF16),
            vmem((BLOCKS, BLOCK, WIDTH), BF16),
            vmem((BLOCKS, BLOCK, QUERY), BF16),
            vmem((BLOCKS, BLOCK, KEYVAL), BF16),
            vmem((2 * PAIRS, both, SPAN), BF16),
            vmem((2 * PAIRS, both, SPAN), F32),
            vmem((both, QUERY), BF16),
            vmem((both, WIDTH), F32),
            vmem((both, WIDTH), F32),
            vmem((both, LANES), F32),
            vmem((both, WIDTH), F32),
            vmem((both, WIDTH), F32),
            vmem((both, QUERY), BF16),
            vmem((TIME, 2 * SPAN, LANES), BF16),
            vmem((WIDTH, 2 * SPAN), BF16),
            vmem((WIDTH, QUERY), BF16),
            vmem((2, NX, *halves), BF16),
            vmem((2, NX, *halves), BF16),
            vmem((2, NX, *halves), BF16),
            vmem(halves, BF16),
            vmem(halves, BF16),
            vmem((2, *halves), BF16),
            vmem((2, *halves), BF16),
            vmem((2, NY, *piece), BF16),
            vmem((2, NY - 1, *piece), BF16),
            vmem((NZ_HI, NZ_LO, PIECE, LANES), F32),
            vmem((NZ_HI * NZ_LO - 1, PIECE, LANES), F32),
            pltpu.SemaphoreType.DMA((13,)),
            pltpu.SemaphoreType.DMA((49,)),
            pltpu.SemaphoreType.DMA((BLOCKS,)),
            pltpu.SemaphoreType.DMA((35,)),
        ],
        compiler_params=pltpu.CompilerParams(
            collective_id=0, has_side_effects=True, vmem_limit_bytes=44 << 20
        ),
        name="layer",
    )(
        *[
            pltpu.with_memory_space_constraint(operand, pltpu.MemorySpace.HBM)
            for operand in (
                utt_blocks,
                block_slot,
                left_count,
                frames,
                out_grad,
                norm1_gain.reshape(1, WIDTH),
                w_query,
                w_kv,
                w_out,
                norm2_gain.reshape(1, WIDTH),
                conv_kernel,
                conv_bias.reshape(1, WIDTH),
            )
        ],
    )


def solution(mesh):
    return jax.shard_map(
        forward,
        mesh=mesh,
        in_specs=(
            P(("dp", "tm"), None),
            P(("dp", "tm"), None),
            P(),
            P(),
            P(),
            P(),
            P(),
            P(),
            P(),
            P("dp", None),
            P("dp", None),
            P("dp", None),
        ),
        out_specs=(P(("dp", "tm"), None), P("dp", "tm")),
        check_vma=False,
    )
```

```python
import jax
import jax.numpy as jnp
from jax import lax
from jax.experimental import pallas as pl
from jax.experimental.pallas import tpu as pltpu
from jax.sharding import PartitionSpec as P

HEADS = 8
HEAD = 64
PAIRS = HEADS // 2
TAPS = 31
BLOCK = 64
BLOCKS = 16
TIME = 8
UTTERANCES = 4
WIDTH = 1024
QUERY = 512
KEYVAL = 1024
LANES = 128
TAIL = 32
ROWS = TAIL + BLOCK
SPAN = 4 * BLOCK
NX, NY, NZ_LO, NZ_HI = 4, 8, 2, 4
PIECE = 16
EPSILON = 1e-05
SOFT_CAP = 4.0
MESH = pl.DeviceIdType.MESH
F32 = jnp.float32
BF16 = jnp.bfloat16


def unit_rows(rows):
    row_mean = jnp.mean(rows, axis=-1, keepdims=True)
    centred = rows - row_mean
    inv = lax.rsqrt(jnp.mean(centred * centred, axis=-1, keepdims=True) + EPSILON)
    return centred * inv, inv


def dot(a, b, dims):
    return lax.dot_general(a, b, (dims, ((), ())), preferred_element_type=F32)


def stack_heads(pair_rows):
    lane = lax.broadcasted_iota(jnp.int32, pair_rows.shape, 1)
    zero = jnp.zeros((), pair_rows.dtype)
    return jnp.concatenate(
        [
            jnp.where(lane < HEAD, pair_rows, zero),
            jnp.where(lane >= HEAD, pair_rows, zero),
        ],
        axis=0,
    )


def layer_kernel(
    lengths_hbm,
    slots_hbm,
    counts_hbm,
    frames_hbm,
    grad_hbm,
    gain1_hbm,
    w_query_hbm,
    w_kv_hbm,
    w_out_hbm,
    gain2_hbm,
    taps_hbm,
    bias_hbm,
    out_ref,
    share_ref,
    lengths_ref,
    slots_ref,
    counts_ref,
    grad_ref,
    gain1_ref,
    w_query_ref,
    w_kv_ref,
    w_out_ref,
    gain2_ref,
    taps_ref,
    bias_ref,
    gath_ref,
    normed_ref,
    query_ref,
    kv_ref,
    probs_ref,
    slope_ref,
    context_ref,
    hidden_ref,
    unit_ref,
    inv_ref,
    conv_ref,
    back_ref,
    grad_context_ref,
    term_ref,
    turned_ref,
    flipped_ref,
    parts_ref,
    pair_ref,
    mine_ref,
    far_up_ref,
    far_down_ref,
    left_ref,
    right_ref,
    plane_ref,
    plane_in_ref,
    line_ref,
    line_in_ref,
    load_sem,
    send_sem,
    slot_sem,
    recv_sem,
):
    dp = lax.axis_index("dp")
    tm = lax.axis_index("tm")
    z_lo, x, y = dp // (NX * NY), (dp // NY) % NX, dp % NY
    z_hi, core = tm // 2, tm % 2
    sibling = z_hi * 2 + 1 - core
    above = ((z_hi + 1) % NZ_HI) * 2 + core
    below = ((z_hi + NZ_HI - 1) % NZ_HI) * 2 + core
    beyond = ((z_hi + 2) % NZ_HI) * 2 + core

    def at(other_z_lo, other_x, other_y):
        return (other_z_lo * NX + other_x) * NY + other_y

    up, down, far = (x + 1) % NX, (x + NX - 1) % NX, (x + 2) % NX
    dp_up, dp_down = at(z_lo, up, y), at(z_lo, down, y)
    plane = [at(z_lo, x, (y + step) % NY) for step in range(1, NY)]

    def line(turn, flip):
        return (
            at((z_lo + flip) % NZ_LO, x, y),
            ((z_hi + turn) % NZ_HI) * 2 + core,
        )

    loads = [
        pltpu.make_async_copy(src, dst, load_sem.at[n])
        for n, (src, dst) in enumerate(
            (
                (frames_hbm.at[pl.ds(0, BLOCK)], gath_ref.at[2 * tm]),
                (frames_hbm.at[pl.ds(BLOCK, BLOCK)], gath_ref.at[2 * tm + 1]),
                (gain1_hbm, gain1_ref),
                (w_query_hbm, w_query_ref),
                (w_kv_hbm, w_kv_ref),
                (w_out_hbm, w_out_ref),
                (gain2_hbm, gain2_ref),
                (taps_hbm, taps_ref),
                (bias_hbm, bias_ref),
                (grad_hbm, grad_ref),
                (lengths_hbm, lengths_ref),
                (slots_hbm, slots_ref),
                (counts_hbm, counts_ref),
            )
        )
    ]
    for copy in loads:
        copy.start()

    partners = [(plane[step - 1], tm) for step in (4, 3, 5, 2, 6, 1, 7)]
    partners += [
        line(turn, flip)
        for turn in (2, 1, 3, 0)
        for flip in (1, 0)
        if turn or flip
    ]
    partners += [(dp_up, tm), (dp_down, tm), (dp, sibling)]
    barrier = pltpu.get_barrier_semaphore()
    for partner in partners:
        pl.semaphore_signal(barrier, inc=1, device_id=partner, device_id_type=MESH)
    pl.semaphore_wait(barrier, len(partners))

    sent = []

    def put(src, dst, arrival, target):
        copy = pltpu.make_async_remote_copy(
            src_ref=src,
            dst_ref=dst,
            send_sem=send_sem.at[len(sent)],
            recv_sem=arrival,
            device_id=target,
            device_id_type=MESH,
        )
        copy.start()
        sent.append(copy)
        return copy

    def pass_on(src, slot, target):
        put(src, gath_ref.at[slot], slot_sem.at[slot], (dp, target))

    def landed(slot):
        pltpu.make_async_remote_copy(
            src_ref=gath_ref.at[slot],
            dst_ref=gath_ref.at[slot],
            send_sem=send_sem.at[0],
            recv_sem=slot_sem.at[slot],
            device_id=(dp, sibling),
            device_id_type=MESH,
        ).wait_recv()

    own = [frames_hbm.at[pl.ds(b * BLOCK, BLOCK)] for b in range(2)]
    pass_on(own[0], 2 * tm, above)
    pass_on(own[1], 2 * tm + 1, below)
    pass_on(own[0], 2 * tm, sibling)
    pass_on(own[1], 2 * tm + 1, sibling)

    def project(source):
        rows = gath_ref[pl.ds(2 * source, 2)].reshape(2 * BLOCK, WIDTH).astype(F32)
        unit, _ = unit_rows(rows)
        normed = (unit * gain1_ref[...]).astype(BF16)
        normed_ref[pl.ds(2 * source, 2)] = normed.reshape(2, BLOCK, WIDTH)
        queries = dot(normed, w_query_ref[...], ((1,), (0,))).astype(BF16)
        query_ref[pl.ds(2 * source, 2)] = queries.reshape(2, BLOCK, QUERY)
        keys_values = dot(normed, w_kv_ref[...], ((1,), (0,))).astype(BF16)
        kv_ref[pl.ds(2 * source, 2)] = keys_values.reshape(2, BLOCK, KEYVAL)

    def other_core(source):
        return source + 1 - 2 * core

    for copy in loads[:5]:
        copy.wait()
    project(tm)
    leading = sent[:2]
    for copy in leading:
        copy.wait_send()
    pass_on(own[1], 2 * tm + 1, above)
    pass_on(own[0], 2 * tm, below)
    landed(2 * sibling)
    landed(2 * sibling + 1)
    project(sibling)
    landed(2 * below)
    pass_on(gath_ref.at[2 * below], 2 * below, above)
    pass_on(gath_ref.at[2 * below], 2 * below, sibling)
    landed(2 * above + 1)
    pass_on(gath_ref.at[2 * above + 1], 2 * above + 1, below)
    pass_on(gath_ref.at[2 * above + 1], 2 * above + 1, sibling)
    landed(2 * below + 1)
    pass_on(gath_ref.at[2 * below + 1], 2 * below + 1, sibling)
    landed(2 * above)
    pass_on(gath_ref.at[2 * above], 2 * above, sibling)
    project(below)
    project(above)
    for copy in loads[5:]:
        copy.wait()
    flipped_ref[...] = w_out_ref[...].T
    for source in (other_core(below), other_core(above)):
        landed(2 * source)
        landed(2 * source + 1)
        project(source)
    landed(2 * beyond)
    pass_on(gath_ref.at[2 * beyond], 2 * beyond, sibling)
    landed(2 * beyond + 1)
    pass_on(gath_ref.at[2 * beyond + 1], 2 * beyond + 1, sibling)
    project(beyond)
    landed(2 * other_core(beyond))
    landed(2 * other_core(beyond) + 1)
    project(other_core(beyond))

    def position(block):
        end, start = jnp.int32(0), jnp.int32(0)
        for u in range(UTTERANCES):
            length = lengths_ref[0, u]
            end = end + length
            start = start + jnp.where(block >= end, length, 0)
        return block - start

    blocks = []
    for i in range(2):
        block = jnp.int32(0)
        for b in range(BLOCKS):
            block = jnp.where(slots_ref[0, b] == 2 * tm + i, b, block)
        before = jnp.maximum(block - 1, 0)
        here, there = position(block), position(before)
        reach = jnp.minimum(counts_ref[0, block], here)
        reach_before = jnp.minimum(counts_ref[0, before], there)
        window = [slots_ref[0, jnp.maximum(block - 3 + lane, 0)] for lane in range(4)]
        blocks.append((reach, reach_before, here >= 1, window))

    def tail_and_own(ref, i, lanes):
        _, _, _, window = blocks[i]
        return jnp.concatenate(
            [ref[window[2], BLOCK - TAIL :, lanes], ref[window[3], :, lanes]], axis=0
        )

    def spanned(ref, i, lanes):
        return jnp.concatenate(
            [ref[slot, :, lanes] for slot in blocks[i][3]], axis=0
        )

    for i in range(2):
        for n in range(2):
            rows = jnp.concatenate(
                [normed_ref[slot] for slot in blocks[i][3][2 * n : 2 * n + 2]], axis=0
            )
            start = i * SPAN + n * LANES
            turned_ref[:, start : start + LANES] = rows.T

    key_lane = lax.broadcasted_iota(jnp.int32, (ROWS, SPAN), 1) // BLOCK
    row = lax.broadcasted_iota(jnp.int32, (ROWS, SPAN), 0)
    lane = lax.broadcasted_iota(jnp.int32, (ROWS, LANES), 1)
    allowed = []
    for i in range(2):
        reach, reach_before, _, _ = blocks[i]
        last = jnp.where(row < TAIL, 2, 3)
        first = last - jnp.where(row < TAIL, reach_before, reach)
        mask = jnp.where((key_lane >= first) & (key_lane <= last), 1.0, 0.0)
        allowed.append(jnp.concatenate([mask, mask], axis=0))

    def pair_columns(pair):
        return (
            slice(pair * LANES, (pair + 1) * LANES),
            slice(QUERY + pair * LANES, QUERY + (pair + 1) * LANES),
        )

    for pair in range(PAIRS):
        columns, value_columns = pair_columns(pair)
        both = range(2)
        q = [stack_heads(tail_and_own(query_ref, i, columns)) for i in both]
        raw = [dot(q[i], spanned(kv_ref, i, columns), ((1,), (1,))) for i in both]
        bent = [jnp.tanh(raw[i] * (1.0 / (SOFT_CAP * 8.0))) for i in both]
        exped = [jnp.exp(SOFT_CAP * bent[i]) * allowed[i] for i in both]
        scale = [1.0 / jnp.sum(exped[i], axis=-1, keepdims=True) for i in both]
        probs = [exped[i] * scale[i] for i in both]
        probs_b = [probs[i].astype(BF16) for i in both]
        heads = [
            dot(probs_b[i], spanned(kv_ref, i, value_columns), ((1,), (0,)))
            for i in both
        ]
        for i in both:
            probs_ref[i * PAIRS + pair] = probs_b[i]
            slope_ref[i * PAIRS + pair] = (
                probs[i] * (1.0 - bent[i] * bent[i]) * 0.125
            )
            context_ref[i * ROWS : (i + 1) * ROWS, columns] = jnp.where(
                lane < HEAD, heads[i][:ROWS], heads[i][ROWS:]
            ).astype(BF16)

    gain2 = gain2_ref[...]
    whole = slice(0, WIDTH)
    projected = dot(context_ref[...], w_out_ref[...], ((1,), (0,)))
    for i in range(2):
        span = slice(i * ROWS, (i + 1) * ROWS)
        hidden = tail_and_own(gath_ref, i, whole).astype(F32) + projected[span]
        hidden_ref[span] = hidden
        unit, inv = unit_rows(hidden)
        unit_ref[span] = unit
        inv_ref[span] = jnp.broadcast_to(inv, (ROWS, LANES))
        conv_in = (unit * gain2).astype(BF16).astype(F32)
        keep = jnp.where(blocks[i][2], 1.0, 0.0)
        conv_ref[i * ROWS : i * ROWS + TAIL] = conv_in[:TAIL] * keep
        conv_ref[i * ROWS + TAIL : (i + 1) * ROWS] = conv_in[TAIL:]

    for i in range(2):
        keep = jnp.where(blocks[i][2], 1.0, 0.0)

        def strip_pass(strip, carry):
            lanes = pl.ds(pl.multiple_of(strip * LANES, LANES), LANES)
            ext = conv_ref[i * ROWS : (i + 1) * ROWS, lanes]
            mixed = jnp.broadcast_to(bias_ref[:, lanes], (BLOCK, LANES))
            for shift in range(8):
                turned = ext if shift == 0 else pltpu.roll(ext, ROWS - shift, axis=0)
                for base in range(0, 40, 8):
                    tap = base + shift - 2
                    if 0 <= tap < TAPS:
                        mixed = (
                            mixed
                            + taps_ref[tap : tap + 1, lanes]
                            * turned[base : base + BLOCK]
                        )
            gate = 1.0 / (1.0 + jnp.exp(-mixed))
            hidden = hidden_ref[i * ROWS + TAIL : (i + 1) * ROWS, lanes]
            out_ref[i * BLOCK : (i + 1) * BLOCK, lanes] = (
                hidden + mixed * gate
            ).astype(BF16)
            out_grad = grad_ref[i * BLOCK : (i + 1) * BLOCK, lanes].astype(F32)
            grad_mixed = out_grad * gate * (1.0 + mixed * (1.0 - gate))
            zeros = jnp.zeros((8, LANES), F32)
            padded = jnp.concatenate([zeros, grad_mixed, zeros], axis=0)
            reached = [jnp.zeros((BLOCK + 8, LANES), F32) for _ in range(4)]
            for shift in range(8):
                turned = (
                    padded
                    if shift == 0
                    else pltpu.roll(padded, BLOCK + 16 - shift, axis=0)
                )[: BLOCK + 8]
                for base in range(4):
                    tap = TAPS - 1 - 8 * base - shift
                    if 0 <= tap < TAPS:
                        reached[base] = (
                            reached[base] + taps_ref[tap : tap + 1, lanes] * turned
                        )
            total = jnp.concatenate(
                [
                    sum(
                        reached[base][row - 24 + 8 * base : row - 16 + 8 * base]
                        for base in range(4)
                        if 0 <= row - 24 + 8 * base < BLOCK + 8
                    )
                    for row in range(0, ROWS, 8)
                ],
                axis=0,
            )
            back_ref[i * ROWS : i * ROWS + TAIL, lanes] = total[:TAIL] * keep
            back_ref[i * ROWS + TAIL : (i + 1) * ROWS, lanes] = total[TAIL:]
            return carry

        lax.fori_loop(0, WIDTH // LANES, strip_pass, 0)

    grad_rows = []
    for i in range(2):
        span = slice(i * ROWS, (i + 1) * ROWS)
        scaled = back_ref[span] * gain2
        unit = unit_ref[span]
        first = jnp.mean(scaled, axis=-1, keepdims=True)
        second = jnp.mean(scaled * unit, axis=-1, keepdims=True)
        grads = inv_ref[span, :1] * (scaled - first - unit * second)
        own_rows = grad_ref[i * BLOCK : (i + 1) * BLOCK].astype(F32)
        grad_rows += [grads[:TAIL].astype(BF16), (grads[TAIL:] + own_rows).astype(BF16)]
    grad_context_ref[...] = dot(
        jnp.concatenate(grad_rows, axis=0), flipped_ref[...], ((1,), (0,))
    ).astype(BF16)

    def pair_of(n, parity):
        return 2 * ((z_hi + n) % 2) + parity

    def differentiate(pair):
        columns = pl.ds(pl.multiple_of(pair * LANES, LANES), LANES)
        value_columns = pl.ds(pl.multiple_of(QUERY + pair * LANES, LANES), LANES)
        both = range(2)
        span = [slice(i * SPAN, (i + 1) * SPAN) for i in both]
        rows = [slice(i * ROWS, (i + 1) * ROWS) for i in both]
        grads = [stack_heads(grad_context_ref[rows[i], columns]) for i in both]
        grad_probs = [
            dot(grads[i], spanned(kv_ref, i, value_columns), ((1,), (1,)))
            for i in both
        ]
        value_terms = [
            dot(probs_ref[i * PAIRS + pair], grads[i], ((0,), (0,))) for i in both
        ]
        context = [context_ref[rows[i], columns].astype(F32) for i in both]
        delta = [
            jnp.sum(
                grads[i].astype(F32) * jnp.concatenate([context[i]] * 2, axis=0),
                axis=-1,
                keepdims=True,
            )
            for i in both
        ]
        grad_raw = [
            (slope_ref[i * PAIRS + pair] * (grad_probs[i] - delta[i])).astype(BF16)
            for i in both
        ]
        q = [stack_heads(tail_and_own(query_ref, i, columns)) for i in both]
        key_terms = [dot(grad_raw[i], q[i], ((0,), (0,))) for i in both]
        for i in both:
            term_ref[PAIRS + pair, span[i]] = value_terms[i].astype(BF16)
            term_ref[pair, span[i]] = key_terms[i].astype(BF16)

    def product(n, parity):
        right = jnp.concatenate(
            [
                term_ref[2 * ((z_hi + n + 2 * m) % NZ_HI) + parity]
                for m in range(2)
            ],
            axis=1,
        )
        return dot(turned_ref[...], right, ((1,), (0,)))

    tiles = [
        (other, m, half)
        for other in range(NX)
        for m in range(2)
        for half in range(NZ_LO)
    ]

    def tile(rows, other, m, half):
        start = (half * NX + other) * LANES
        return rows[start : start + LANES, m * LANES : (m + 1) * LANES]

    def share_pair(n):
        differentiate(pair_of(n, 1 - core))
        rows = product(n, 1 - core)
        for other, m, half in tiles:
            parts_ref[n, other, m, half] = tile(rows, other, m, half).astype(BF16)
        return put(parts_ref.at[n], pair_ref.at[n], recv_sem.at[n], (dp, sibling))

    def add_pair(n, shared):
        differentiate(pair_of(n, core))
        rows = product(n, core)
        shared.wait_recv()
        for other, m, half in tiles:
            mine_ref[n, other, m, half] = (
                tile(rows, other, m, half) + pair_ref[n, other, m, half].astype(F32)
            ).astype(BF16)

    def start_ring(n):
        return (
            put(mine_ref.at[n, far, 0], far_up_ref.at[n], recv_sem.at[2 + n], (dp_up, tm)),
            put(
                mine_ref.at[n, far, 1],
                far_down_ref.at[n],
                recv_sem.at[4 + n],
                (dp_down, tm),
            ),
            put(mine_ref.at[n, up, 1], left_ref.at[n, 1], recv_sem.at[6 + n], (dp_up, tm)),
            put(
                mine_ref.at[n, down, 0],
                right_ref.at[n, 0],
                recv_sem.at[8 + n],
                (dp_down, tm),
            ),
        )

    def end_ring(n, ring):
        ring[0].wait_recv()
        mine_ref[n, up, 0] = (
            mine_ref[n, up, 0].astype(F32) + far_up_ref[n].astype(F32)
        ).astype(BF16)
        left = put(
            mine_ref.at[n, up, 0], left_ref.at[n, 0], recv_sem.at[10 + n], (dp_up, tm)
        )
        ring[1].wait_recv()
        mine_ref[n, down, 1] = (
            mine_ref[n, down, 1].astype(F32) + far_down_ref[n].astype(F32)
        ).astype(BF16)
        right = put(
            mine_ref.at[n, down, 1],
            right_ref.at[n, 1],
            recv_sem.at[12 + n],
            (dp_down, tm),
        )
        return ring[2], ring[3], left, right

    shared = share_pair(0)
    add_pair(0, shared)
    ring_first = start_ring(0)
    shared = share_pair(1)
    add_pair(1, shared)
    ring_second = start_ring(1)
    rings = [end_ring(0, ring_first), end_ring(1, ring_second)]

    arrivals = 14
    in_plane = []
    farthest_first = (4, 3, 5, 2, 6, 1, 7)
    for n in range(2):
        for copy in rings[n]:
            copy.wait_recv()
        for m in range(2):
            total = (
                mine_ref[n, x, m].astype(F32)
                + left_ref[n, m].astype(F32)
                + right_ref[n, m].astype(F32)
            ).astype(BF16)
            for other in range(NY):
                plane_ref[n, other, m] = total[
                    :, other * PIECE : (other + 1) * PIECE
                ]
        in_plane.append(
            [
                put(
                    plane_ref.at[n, (y + step) % NY],
                    plane_in_ref.at[n, step - 1],
                    recv_sem.at[arrivals + n * (NY - 1) + step - 1],
                    (plane[step - 1], tm),
                )
                for step in farthest_first
            ]
        )
    arrivals += 2 * (NY - 1)
    in_line = []
    for n in range(2):
        summed = plane_ref[n, y].astype(F32)
        for copy, step in reversed(list(zip(in_plane[n], farthest_first))):
            copy.wait_recv()
            summed = summed + plane_in_ref[n, step - 1].astype(F32)
        for m in range(2):
            turn = 2 * m + n
            line_ref[turn] = summed[m]
            for flip in range(NZ_LO):
                number = 2 * turn + flip - 1
                if number >= 0:
                    in_line.append(
                        put(
                            line_ref.at[turn, (z_lo + flip) % NZ_LO],
                            line_in_ref.at[number],
                            recv_sem.at[arrivals + number],
                            line(turn, flip),
                        )
                    )
    for copy in in_line:
        copy.wait_recv()
    summed = line_ref[0, z_lo]
    for number in range(NZ_HI * NZ_LO - 1):
        summed = summed + line_in_ref[number]
    share_ref[...] = summed
    for copy in sent[2:]:
        copy.wait_send()


def forward(
    frames,
    out_grad,
    norm1_gain,
    w_query,
    w_kv,
    w_out,
    norm2_gain,
    conv_kernel,
    conv_bias,
    utt_blocks,
    block_slot,
    left_count,
):
    hbm = pl.BlockSpec(memory_space=pltpu.MemorySpace.HBM)
    both = 2 * ROWS
    halves = (2, NZ_LO, LANES, LANES)
    piece = (2, NZ_LO, PIECE, LANES)
    vmem = pltpu.VMEM
    return pl.pallas_call(
        layer_kernel,
        out_shape=(
            jax.ShapeDtypeStruct((2 * BLOCK, WIDTH), BF16),
            jax.ShapeDtypeStruct((PIECE, LANES), F32),
        ),
        in_specs=[hbm] * 12,
        out_specs=(pl.BlockSpec(memory_space=pltpu.VMEM),) * 2,
        scratch_shapes=[
            pltpu.SMEM((1, UTTERANCES), jnp.int32),
            pltpu.SMEM((1, BLOCKS), jnp.int32),
            pltpu.SMEM((1, BLOCKS), jnp.int32),
            vmem((2 * BLOCK, WIDTH), BF16),
            vmem((1, WIDTH), F32),
            vmem((WIDTH, QUERY), BF16),
            vmem((WIDTH, KEYVAL), BF16),
            vmem((QUERY, WIDTH), BF16),
            vmem((1, WIDTH), F32),
            vmem((TAPS, WIDTH), F32),
            vmem((1, WIDTH), F32),
            vmem((BLOCKS, BLOCK, WIDTH), BF16),
            vmem((BLOCKS, BLOCK, WIDTH), BF16),
            vmem((BLOCKS, BLOCK, QUERY), BF16),
            vmem((BLOCKS, BLOCK, KEYVAL), BF16),
            vmem((2 * PAIRS, both, SPAN), BF16),
            vmem((2 * PAIRS, both, SPAN), F32),
            vmem((both, QUERY), BF16),
            vmem((both, WIDTH), F32),
            vmem((both, WIDTH), F32),
            vmem((both, LANES), F32),
            vmem((both, WIDTH), F32),
            vmem((both, WIDTH), F32),
            vmem((both, QUERY), BF16),
            vmem((TIME, 2 * SPAN, LANES), BF16),
            vmem((WIDTH, 2 * SPAN), BF16),
            vmem((WIDTH, QUERY), BF16),
            vmem((2, NX, *halves), BF16),
            vmem((2, NX, *halves), BF16),
            vmem((2, NX, *halves), BF16),
            vmem(halves, BF16),
            vmem(halves, BF16),
            vmem((2, *halves), BF16),
            vmem((2, *halves), BF16),
            vmem((2, NY, *piece), BF16),
            vmem((2, NY - 1, *piece), BF16),
            vmem((NZ_HI, NZ_LO, PIECE, LANES), F32),
            vmem((NZ_HI * NZ_LO - 1, PIECE, LANES), F32),
            pltpu.SemaphoreType.DMA((13,)),
            pltpu.SemaphoreType.DMA((49,)),
            pltpu.SemaphoreType.DMA((BLOCKS,)),
            pltpu.SemaphoreType.DMA((35,)),
        ],
        compiler_params=pltpu.CompilerParams(
            collective_id=0, has_side_effects=True, vmem_limit_bytes=44 << 20
        ),
        name="layer",
    )(
        *[
            pltpu.with_memory_space_constraint(operand, pltpu.MemorySpace.HBM)
            for operand in (
                utt_blocks,
                block_slot,
                left_count,
                frames,
                out_grad,
                norm1_gain.reshape(1, WIDTH),
                w_query,
                w_kv,
                w_out,
                norm2_gain.reshape(1, WIDTH),
                conv_kernel,
                conv_bias.reshape(1, WIDTH),
            )
        ],
    )


def solution(mesh):
    return jax.shard_map(
        forward,
        mesh=mesh,
        in_specs=(
            P(("dp", "tm"), None),
            P(("dp", "tm"), None),
            P(),
            P(),
            P(),
            P(),
            P(),
            P(),
            P(),
            P("dp", None),
            P("dp", None),
            P("dp", None),
        ),
        out_specs=(P(("dp", "tm"), None), P("dp", "tm")),
        check_vma=False,
    )
```
